32 devices in a mesh: lon: 8 (over z, y), rad: 4 (over x, core).
Axes of the slice: x: 2, y: 2, z: 4, core: 2. Of those that a mesh axis runs over, the one named last changes fastest.
Arguments:
- adjoint_temp: float32 [32, 256, 128], P('rad', 'lon'), may hold values from -6 to 6
- viscosity: float32 [32, 256, 128], P('rad', 'lon'), may hold values from 0.1 to 10
- velocity: float32 [3, 32, 256, 128], P(None, 'rad', 'lon'), may hold values from -6 to 6
- misfit_force: float32 [3, 32, 256, 128], P(None, 'rad', 'lon'), may hold values from -6 to 6
- adjoint_guess: float32 [3, 32, 256, 128], P(None, 'rad', 'lon'), may hold values from -3 to 3
Outputs:
- temp_next: float32 [32, 256, 128], P('rad', 'lon')
- adjoint_vel: float32 [3, 32, 256, 128], P(None, 'rad', 'lon')
The draws below stay inside these ranges and needn't reach their ends.
All inputs are finite; a program needn't handle non-finite values.
Results may differ from the reference program's by a relative error of at most 0.00002.
Values sent between devices are 32-bit elements; how exact they have to be, the bound alone decides.
A program may use at most 128 MiB of HBM per device.

```python
import math
import jax
import jax.numpy as jnp

LAT = 128
NU = 2
NC = 8
NR = 32
NL = 256


def block_scale(own_key, dims, shards, least, largest):
    loudness = 1.0
    for axis_at, shards_of in shards:
        steps = jax.random.uniform(jax.random.fold_in(jax.random.fold_in(own_key, 6), axis_at), (shards_of,), jnp.float32, least / len(shards), largest / len(shards))
        loudness = loudness * jnp.repeat(jnp.exp(steps), dims[axis_at] // shards_of).reshape((-1,) + (1,) * (len(dims) - 1 - axis_at))
    return loudness


def bell_draw(key, shape, scale, bound, pieces=(), kind=jnp.bfloat16):
    level = block_scale(key, shape, pieces, -0.22, 0.18) if pieces else 1.0
    result = jax.random.normal(key, shape, jnp.float32) * scale * level
    return jnp.minimum(jnp.maximum(result, -bound), bound).astype(kind)


def setup_inputs(seed: int = 0) -> dict:
    streams_of = jax.random.split(jax.random.key(seed), 6)
    return {
        "adjoint_temp": bell_draw(streams_of[0], (NR, NL, LAT), 1.0, 6.0, ((0, 4), (1, 8)), jnp.float32),
        "viscosity": jnp.clip(jnp.exp(math.log(10.0) - 4.6051702 * jax.random.uniform(streams_of[1], (NR, NL, LAT), jnp.float32) ** block_scale(streams_of[1], (NR, NL, LAT), ((0, 4), (1, 8)), -0.2, 0.2)), 0.1, 10.0),
        "velocity": bell_draw(streams_of[2], (3, NR, NL, LAT), 1.0, 6.0, ((1, 4), (2, 8)), jnp.float32),
        "misfit_force": bell_draw(streams_of[3], (3, NR, NL, LAT), 1.0, 6.0, ((1, 4), (2, 8)), jnp.float32),
        "adjoint_guess": bell_draw(streams_of[4], (3, NR, NL, LAT), 0.5, 3.0, ((1, 4), (2, 8)), jnp.float32),
    }


def shift_zero(x, axis, lower):
    size = x.shape[axis]
    zero = jnp.zeros_like(jax.lax.slice_in_dim(x, 0, 1, axis=axis))
    if lower:
        return jnp.concatenate([zero, jax.lax.slice_in_dim(x, 0, size - 1, axis=axis)], axis=axis)
    return jnp.concatenate([jax.lax.slice_in_dim(x, 1, size, axis=axis), zero], axis=axis)


def neighbours(x):
    west = jnp.roll(x, 1, axis=2)
    east = jnp.roll(x, -1, axis=2)
    down = shift_zero(x, 1, True)
    upper = shift_zero(x, 1, False)
    south = shift_zero(x, 3, True)
    north = shift_zero(x, 3, False)
    return [west, east, down, upper, south, north]


def face_coefs(visc, near):
    coefs = [(visc + item) * 0.5 for item in near]
    diag = coefs[0] + coefs[1] + coefs[2] + coefs[3] + coefs[4] + coefs[5]
    return coefs, diag


def apply_op(field, coefs, diag, scale):
    near = neighbours(field)
    total = coefs[0] * near[0] + coefs[1] * near[1] + coefs[2] * near[2]
    total = total + coefs[3] * near[3] + coefs[4] * near[4] + coefs[5] * near[5]
    return scale * (diag * field - total)


def restrict(x):
    comps, rows, cols, width = x.shape
    return x.reshape(comps, rows // 2, 2, cols // 2, 2, width // 2, 2).mean(axis=(2, 4, 6))


def prolong(x):
    return jnp.repeat(jnp.repeat(jnp.repeat(x, 2, axis=1), 2, axis=2), 2, axis=3)


def reference(adjoint_temp, viscosity, velocity, misfit_force, adjoint_guess):
    both = jnp.stack([adjoint_temp, viscosity])
    near = neighbours(both)
    temp = both[0]
    tn = [item[0] for item in near]
    advect = velocity[0] * (tn[3] - tn[2]) + velocity[1] * (tn[1] - tn[0]) + velocity[2] * (tn[5] - tn[4])
    spread = tn[0] + tn[1] + tn[2] + tn[3] + tn[4] + tn[5] - 6.0 * temp
    temp_next = temp + 0.25 * advect * 0.5 + 0.1 * spread
    visc = both[1:2]
    coefs, diag = face_coefs(visc, [item[1:2] for item in near])
    rhs = misfit_force.at[0].add(temp_next)
    field = adjoint_guess
    for sweep in range(NU):
        field = field + 0.8 * (rhs - apply_op(field, coefs, diag, 1.0)) / diag
    coarse_res = restrict(rhs - apply_op(field, coefs, diag, 1.0))
    coarse_visc = restrict(visc)
    ccoefs, cdiag = face_coefs(coarse_visc, neighbours(coarse_visc))
    corr = jnp.zeros_like(coarse_res)
    for sweep in range(NC):
        corr = corr + 0.8 * (coarse_res - apply_op(corr, ccoefs, cdiag, 0.25)) / (0.25 * cdiag)
    field = field + prolong(corr)
    for sweep in range(NU):
        field = field + 0.8 * (rhs - apply_op(field, coefs, diag, 1.0)) / diag
    return temp_next, field
```

```python
import functools

import jax
import jax.numpy as jnp
from jax import lax
from jax.experimental import pallas as pl
from jax.experimental.pallas import tpu as pltpu
from jax.sharding import PartitionSpec as P

NU = 2
NC = 8
PAD = 8
DEEP = 3
MESH = pl.DeviceIdType.MESH


def kernel(ni, nj, temp_hbm, visc_hbm, vel_hbm, mis_hbm, guess_hbm, tn_ref, out_ref,
           vel_ref, mis_ref, local,
           W0, U1, U2, U3, U4, WT, B, D, INV, RS, RV, CP, CV, GO, GW, GE, CG, CW, CB, EA, EB, EX,
           S0, L0, SC, LC, SX, LX, LR, SD, LD, send, recv):
    R, C, LAT = temp_hbm.shape
    half = R // 4
    cols = C // 2
    strip = PAD
    rows = 2 * half
    i = lax.axis_index("lon")
    j = lax.axis_index("rad")
    west, east = lax.rem(i + ni - 1, ni), lax.rem(i + 1, ni)

    q = lambda r: r + DEEP
    mid = pl.ds(PAD, C)
    inner = pl.ds(DEEP, R)
    loads = [
        pltpu.make_async_copy(visc_hbm, W0.at[4, inner, mid], local.at[0]),
        pltpu.make_async_copy(temp_hbm, W0.at[3, inner, mid], local.at[1]),
        pltpu.make_async_copy(guess_hbm, W0.at[0:3, inner, mid], local.at[2]),
        pltpu.make_async_copy(vel_hbm, vel_ref, local.at[3]),
        pltpu.make_async_copy(mis_hbm, mis_ref, local.at[4]),
    ]
    for item in loads:
        item.start()

    barrier = pltpu.get_barrier_semaphore()
    for d in range(nj):
        other = lax.rem(j + d, nj)
        for lon in (west, east) if d == 0 else (west, east, i):
            pl.semaphore_signal(barrier, inc=1, device_id={"lon": lon, "rad": other}, device_id_type=MESH)

    lo, hi = PAD // 2, C + PAD + PAD // 2
    span = hi - lo
    lane = lax.broadcasted_iota(jnp.int32, (span, LAT), 1)
    first, last = lane == 0, lane == LAT - 1
    even = lax.rem(lane, 2) == 0

    edges = (pl.ds(0, PAD), pl.ds(PAD + C, PAD))
    for edge in edges:
        W0[4, :, edge, :] = jnp.ones_like(W0[4, :, edge, :])
        for buf in (B, U1, U2):
            buf[:, :, edge, :] = jnp.zeros_like(buf[:, :, edge, :])
    for c in range(3):
        for r in (0, R + 1):
            B[c, r, mid, :] = jnp.zeros((C, LAT), jnp.float32)
        for r in (-2, -1, R, R + 1):
            U1[c, q(r), mid, :] = jnp.zeros((C, LAT), jnp.float32)
        for r in (-2, R + 1):
            U2[c, q(r), mid, :] = jnp.zeros((C, LAT), jnp.float32)
    for buf in (GO, GW, GE):
        for place in (0, nj + 1):
            buf[place, :, 2] = jnp.zeros_like(buf[place, :, 2])
    top = half * nj + 1
    for buf in (EA, EB):
        buf[...] = jnp.zeros_like(buf)
    CG[0, 0] = jnp.zeros_like(CG[0, 0])
    CG[0, top] = jnp.zeros_like(CG[0, top])

    def halves(a, b):
        a = a + pltpu.roll(a, LAT - 1, 1)
        b = b + pltpu.roll(b, 1, 1)
        return 0.125 * jnp.where(even[: a.shape[0]], a, b)

    def under(cond, action):
        if cond is None:
            action()
        else:
            pl.when(cond)(action)

    class Copy:
        def __init__(self, slot, src, dst, lon, rad, to=None, came=None):
            self.item = pltpu.make_async_remote_copy(
                src_ref=src, dst_ref=dst, send_sem=send.at[slot], recv_sem=recv.at[slot],
                device_id={"lon": lon, "rad": rad}, device_id_type=MESH)
            self.to, self.came = to, came

        def start(self):
            under(self.to, self.item.start)

        def arrive(self):
            under(self.came, self.item.wait_recv)

        def leave(self):
            under(self.to, self.item.wait_send)

    inside = lambda d: (None if d == 0 else (j + d >= 0) & (j + d < nj))
    corners = [(di, dj) for di in (-1, 1) for dj in (-1, 1)]
    at_lon = {-1: west, 0: i, 1: east}

    loads[0].wait()
    for p in range(rows):
        RV[p] = W0[4, q(2 * p), mid, :] + W0[4, q(2 * p + 1), mid, :]
    for r in range(half):
        a = RV[r, pl.ds(0, cols, 2), :] + RV[r, pl.ds(1, cols, 2), :]
        b = RV[r + half, pl.ds(0, cols, 2), :] + RV[r + half, pl.ds(1, cols, 2), :]
        CV[0, r] = halves(a, b)
    for n in range(3):
        S0[0, 4 + n] = W0[4, inner, PAD + n, :]
        S0[1, 4 + n] = W0[4, inner, PAD + C - 1 - n, :]
    for n, (di, dj) in enumerate(corners):
        r0, c0 = (0 if dj < 0 else R - 1), PAD + (0 if di < 0 else C - 1)
        SC[n, 0:1] = W0[4, q(r0), c0 : c0 + 1, :]
        SC[n, 1:2] = W0[4, q(r0), c0 - di : c0 - di + 1, :]
        SC[n, 2:3] = W0[4, q(r0 - dj), c0 : c0 + 1, :]
    loads[1].wait()
    loads[2].wait()
    for c in range(4):
        S0[0, c] = W0[c, inner, PAD, :]
        S0[1, c] = W0[c, inner, PAD + C - 1, :]
    pl.semaphore_wait(barrier, 3 * nj - 1)

    round0 = [
        Copy(0, S0.at[0], L0.at[1], west, j),
        Copy(1, S0.at[1], L0.at[0], east, j),
        Copy(2, W0.at[:, q(0), mid], W0.at[:, q(R), mid], i, j - 1, inside(-1), inside(1)),
        Copy(3, W0.at[:, q(R - 1), mid], W0.at[:, q(-1), mid], i, j + 1, inside(1), inside(-1)),
    ]
    for n, (di, dj) in enumerate(corners):
        round0.append(Copy(4 + n, SC.at[n], LC.at[n], at_lon[di], j + dj, inside(dj), inside(-dj)))
    round0 += [
        Copy(8, W0.at[4, pl.ds(q(1), 2), mid], W0.at[4, pl.ds(q(R + 1), 2), mid], i, j - 1, inside(-1), inside(1)),
        Copy(9, W0.at[4, pl.ds(q(R - 3), 2), mid], W0.at[4, pl.ds(q(-3), 2), mid], i, j + 1, inside(1), inside(-1)),
    ]
    for item in round0:
        item.start()

    def spread(slot, make):
        copies = {}
        for di in (-1, 0, 1):
            copies[di] = []
            for dj in sorted(range(1 - nj, nj), key=abs):
                pair = None if di == 0 and dj == 0 else make(di, dj)
                if pair is not None:
                    copies[di].append(Copy(slot, *pair, at_lon[di], j + dj, inside(dj), inside(-dj)))
                slot = slot + 1
        odd = lax.rem(i, 2) == 1

        def begin(which):
            def action():
                for item in copies[which]:
                    item.start()
            return action

        pl.when(jnp.logical_not(odd))(begin(-1))
        pl.when(odd)(begin(1))
        begin(0)()
        pl.when(odd)(begin(-1))
        pl.when(jnp.logical_not(odd))(begin(1))
        return copies[-1] + copies[0] + copies[1]

    def visc_part(di, dj):
        width = min(NC + 1, NC + 1 - rows * (abs(dj) - 1))
        places = pl.ds(1 + half * j, half)
        if width <= 0:
            return None
        if di == 0:
            return CV, CG.at[:, places, pl.ds(2 * strip, cols)]
        if di < 0:
            return CV.at[:, :, pl.ds(0, width)], CG.at[:, places, pl.ds(2 * strip + cols, width)]
        return CV.at[:, :, pl.ds(cols - width, width)], CG.at[:, places, pl.ds(2 * strip - width, width)]

    coarse_visc = spread(10, visc_part)
    for r in range(half):
        CG[0, 1 + half * j + r, 2 * strip : 2 * strip + cols, :] = CV[0, r]
    loads[3].wait()
    loads[4].wait()

    for item in round0:
        item.arrive()
    for c in range(4):
        W0[c, inner, PAD - 1, :] = L0[0, c]
        W0[c, inner, PAD + C, :] = L0[1, c]
    for n in range(3):
        W0[4, inner, PAD - 1 - n, :] = L0[0, 4 + n]
        W0[4, inner, PAD + C + n, :] = L0[1, 4 + n]
    for n, (di, dj) in enumerate(corners):
        rr, cc = (R if dj < 0 else -1), PAD + (C if di < 0 else -1)
        def place_corner(n=n, di=di, dj=dj, rr=rr, cc=cc):
            W0[4, q(rr), cc : cc + 1, :] = LC[n, 0:1]
            W0[4, q(rr), cc - di : cc - di + 1, :] = LC[n, 1:2]
            W0[4, q(rr - dj), cc : cc + 1, :] = LC[n, 2:3]
        pl.when(inside(-dj))(place_corner)

    @pl.when(j == 0)
    def _():
        W0[:, q(-1)] = jnp.zeros_like(W0[:, q(-1)])
        W0[4, q(-3) : q(-1)] = jnp.ones_like(W0[4, q(-3) : q(-1)])

    @pl.when(j == nj - 1)
    def _():
        W0[:, q(R)] = jnp.zeros_like(W0[:, q(R)])
        W0[4, q(R + 1) : q(R + 3)] = jnp.ones_like(W0[4, q(R + 1) : q(R + 3)])

    def near(buf, c, r, lo=PAD, width=C):
        hi = lo + width
        x = buf[c, q(r), lo:hi, :]
        return x, [
            buf[c, q(r), lo - 1 : hi - 1, :],
            buf[c, q(r), lo + 1 : hi + 1, :],
            buf[c, q(r - 1), lo:hi, :],
            buf[c, q(r + 1), lo:hi, :],
            pltpu.roll(x, 1, 1),
            pltpu.roll(x, LAT - 1, 1),
        ]

    def faces(r):
        v, vn = near(W0, 4, r, lo, span)
        vn[4] = jnp.where(first, 0.0, vn[4])
        vn[5] = jnp.where(last, 0.0, vn[5])
        coefs = [(v + item) * 0.5 for item in vn]
        diag = coefs[0] + coefs[1] + coefs[2] + coefs[3] + coefs[4] + coefs[5]
        return coefs, diag, 0.8 / diag

    for r in range(-1, R + 1):
        coefs, diag, inv = faces(r)
        coefs[4] = jnp.where(first, 0.0, coefs[4])
        coefs[5] = jnp.where(last, 0.0, coefs[5])
        for k in range(6):
            WT[k, r + 1, lo:hi, :] = coefs[k] * inv
        D[r + 1, lo:hi, :] = diag * 1.25
        INV[r + 1, lo:hi, :] = inv

    for r in range(R):
        inv = INV[r + 1, mid, :]
        t, tn = near(W0, 3, r)
        tn[4] = jnp.where(first[:C], 0.0, tn[4])
        tn[5] = jnp.where(last[:C], 0.0, tn[5])
        advect = vel_ref[0, r] * (tn[3] - tn[2]) + vel_ref[1, r] * (tn[1] - tn[0]) + vel_ref[2, r] * (tn[5] - tn[4])
        spread_t = tn[0] + tn[1] + tn[2] + tn[3] + tn[4] + tn[5] - 6.0 * t
        t_next = t + 0.125 * advect + 0.1 * spread_t
        tn_ref[r] = t_next
        B[0, r + 1, mid, :] = (mis_ref[0, r] + t_next) * inv
        B[1, r + 1, mid, :] = mis_ref[1, r] * inv
        B[2, r + 1, mid, :] = mis_ref[2, r] * inv

    @pl.when(j == 0)
    def _():
        WT[2, 1] = jnp.zeros_like(WT[2, 1])
        WT[:, 0] = jnp.zeros_like(WT[:, 0])

    @pl.when(j == nj - 1)
    def _():
        WT[3, R] = jnp.zeros_like(WT[3, R])
        WT[:, R + 1] = jnp.zeros_like(WT[:, R + 1])

    def change(buf, c, r, lo=PAD, width=C):
        x, xn = near(buf, c, r, lo, width)
        t = B[c, r + 1, lo : lo + width, :] - 0.8 * x
        for k in range(6):
            t = t + WT[k, r + 1, lo : lo + width, :] * xn[k]
        return x, t

    for r in range(R):
        for c in range(3):
            x, t = change(W0, c, r)
            U1[c, q(r), mid, :] = x + t

    for c in range(3):
        U2[c, q(-1), mid, :] = WT[3, 0, mid, :] * U1[c, q(0), mid, :]
        U2[c, q(R), mid, :] = WT[2, R + 1, mid, :] * U1[c, q(R - 1), mid, :]
    for r in range(R):
        for c in range(3):
            x, t = change(U1, c, r, lo, span)
            U2[c, q(r), lo:hi, :] = x + t

    def residual(c, r):
        x, t = change(U2, c, r, lo, span)
        U3[c, q(r), lo:hi, :] = x + t
        return D[r + 1, lo:hi, :] * t

    for r, k, p in ((-2, 3, 0), (R + 1, 2, rows + 1)):
        coefs, diag, inv = faces(r)
        other = -1 if r < 0 else R
        for c in range(3):
            t = coefs[k] * U2[c, q(other), lo:hi, :]
            U3[c, q(r), lo:hi, :] = t * inv
            RS[c, p] = t + residual(c, other)
    for p in range(rows):
        for c in range(3):
            RS[c, p + 1] = residual(c, 2 * p) + residual(c, 2 * p + 1)
    wide_c = span // 2
    for c in range(3):
        pair = lambda p: RS[c, p + 1, pl.ds(0, wide_c, 2), :] + RS[c, p + 1, pl.ds(1, wide_c, 2), :]
        for r, a, b in [(r, r, r + half) for r in range(half)] + [(half, rows, -1)]:
            CP[c, r, strip - 2 : strip - 2 + wide_c, :] = halves(pair(a), pair(b))

    def part(di, dj):
        reach = min(NC, NC + 1 - rows * (abs(dj) - 1))
        if reach <= 0:
            return None
        which = pl.ds(0, half + 1) if NC - rows * (abs(dj) - 1) > 0 else pl.ds(half, 1)
        width = reach + 1
        if di == 0:
            take = pl.ds(strip - 1, cols + 2)
            return CP.at[:, which, take], GO.at[j + 1, :, which, take]
        if di < 0:
            return CP.at[:, which, pl.ds(strip - 1, width)], GE.at[j + 1, :, which, pl.ds(strip - 1 + cols, width)]
        begin = strip + cols + 1 - width
        return CP.at[:, which, pl.ds(begin, width)], GW.at[j + 1, :, which, pl.ds(begin - cols, width)]

    slot = 10 + 3 * (2 * nj - 1)
    coarse_res = spread(slot, part)
    slot = slot + 3 * (2 * nj - 1)

    near_cells = lambda di, dj: [(0, 1), (0, 2), (1, 1), (1, 0), (2, 0)]
    for n in range(3):
        for c in range(3):
            SX[0, 3 * n + c] = U3[c, q(-1) : q(R + 1), PAD - n, :]
            SX[1, 3 * n + c] = U3[c, q(-1) : q(R + 1), PAD + C - 1 + n, :]
    for n, (di, dj) in enumerate(corners):
        r0, c0 = (0 if dj < 0 else R - 1), PAD + (0 if di < 0 else C - 1)
        for m, (a, b) in enumerate(near_cells(di, dj)):
            for c in range(3):
                at = c0 + di * b
                SD[n, 3 * m + c : 3 * m + c + 1] = U3[c, q(r0 + dj * a), at : at + 1, :]
    band = pl.ds(PAD - 1, C + 2)
    fine = [
        Copy(slot, SX.at[0], LX.at[1], west, j),
        Copy(slot + 1, SX.at[1], LX.at[0], east, j),
        Copy(slot + 2, U3.at[:, pl.ds(q(-2), 3), band], LR.at[1, :, :, band], i, j - 1, inside(-1), inside(1)),
        Copy(slot + 3, U3.at[:, pl.ds(q(R - 1), 3), band], LR.at[0, :, :, band], i, j + 1, inside(1), inside(-1)),
    ]
    for n, (di, dj) in enumerate(corners):
        fine.append(Copy(slot + 4 + n, SD.at[n], LD.at[n], at_lon[di], j + dj, inside(dj), inside(-dj)))
    for item in fine:
        item.start()

    for item in coarse_visc:
        item.arrive()

    lane_c = lane[:C]

    def coarse_near(buf, c, at, r, lo=PAD, width=None):
        width = width or C
        part = even[:width]
        p = 1 + half * at + r
        block = lambda place, off=0: buf[c, place, lo + off : lo + off + width, :]
        x = block(p)
        if r > 0:
            below = block(p - 1)
        else:
            below = jnp.where(part, pltpu.roll(block(p - 1), LAT - 1, 1), pltpu.roll(block(p + half - 1), 1, 1))
        if r < half - 1:
            above = block(p + 1)
        else:
            above = jnp.where(part, pltpu.roll(block(p - half + 1), LAT - 1, 1), pltpu.roll(block(p + 1), 1, 1))
        return x, [block(p, -1), block(p, 1), below, above, pltpu.roll(x, 2, 1), pltpu.roll(x, LAT - 2, 1)]

    for at in range(nj):
        for r in range(half):
            v, vn = coarse_near(CG, 0, at, r)
            vn[4] = jnp.where(lane_c < 2, 0.0, vn[4])
            vn[5] = jnp.where(lane_c >= LAT - 2, 0.0, vn[5])
            coefs = [(v + item) * 0.5 for item in vn]
            diag = coefs[0] + coefs[1] + coefs[2] + coefs[3] + coefs[4] + coefs[5]
            inv = 0.8 / diag
            coefs[4] = jnp.where(lane_c < 2, 0.0, coefs[4])
            coefs[5] = jnp.where(lane_c >= LAT - 2, 0.0, coefs[5])
            for k in range(6):
                CW[k, half * at + r] = coefs[k] * inv
            CW[6, half * at + r] = 4.0 * inv

    for r in range(half + 1):
        for c in range(3):
            GO[j + 1, c, r] = CP[c, r]
    for item in coarse_res:
        item.arrive()

    col = lax.broadcasted_iota(jnp.int32, (C, LAT), 0)
    own = (col >= strip - 1) & (col <= strip + cols)
    before, after = col <= strip, col >= strip + cols - 1

    def total(s, c, p):
        x = jnp.where(own, GO[s + 1, c, p], 0.0)
        return x + jnp.where(before, GW[s + 1, c, p], 0.0) + jnp.where(after, GE[s + 1, c, p], 0.0)

    even_c = even[:C]
    for s in range(nj):
        for c in range(3):
            for r in range(half):
                b = total(s, c, r)
                if r == 0:
                    b = b + jnp.where(even_c, total(s - 1, c, half), 0.0)
                if r == half - 1:
                    b = b + jnp.where(even_c, 0.0, total(s + 1, c, half))
                p = half * s + r
                b = b * CW[6, p]
                CB[c, p] = b
                EA[c, p + 1, PAD : PAD + C, :] = b

    def coarse_sweep(src, dst, rim):
        near_rim = 2 * rim <= PAD and cols % 8 == 0
        lo = 2 * strip - PAD // 2 if near_rim else PAD
        width = cols + PAD if near_rim else C
        reach = -(-rim // (2 * half))

        def body(at, carry):
            for r in range(half):
                p = half * at + r
                for c in range(3):
                    x, xn = coarse_near(src, c, at, r, lo, width)
                    t = CB[c, p, lo - PAD : lo - PAD + width, :] + 0.2 * x
                    for k in range(6):
                        t = t + CW[k, p, lo - PAD : lo - PAD + width, :] * xn[k]
                    dst[c, p + 1, lo : lo + width, :] = t
            return carry

        if reach > 1:
            lax.fori_loop(0, nj, body, 0, unroll=True)
        else:
            lax.fori_loop(jnp.maximum(j - reach, 0), jnp.minimum(j + reach + 1, nj), body, 0)

    src, dst = EA, EB
    for number in range(NC - 1):
        coarse_sweep(src, dst, NC - 1 - number)
        src, dst = dst, src

    wide = EX.shape[2] // 2
    start = 2 * strip - PAD // 2
    even_wide = lax.rem(lax.broadcasted_iota(jnp.int32, (wide, LAT), 1), 2) == 0
    for c in range(3):
        for m in range(-1, 2 * half + 1):
            low = 0 <= m < half or m == 2 * half
            place = 1 + half * j + {-1: -1, 2 * half: half}.get(m, m % half)
            x = src[c, place, start : start + wide, :]
            if low:
                x = jnp.where(even_wide, x, pltpu.roll(x, 1, 1))
            else:
                x = jnp.where(even_wide, pltpu.roll(x, LAT - 1, 1), x)
            EX[c, m + 1, pl.ds(0, wide, 2), :] = x
            EX[c, m + 1, pl.ds(1, wide, 2), :] = x
    for item in fine:
        item.arrive()
        item.leave()
    for n in range(3):
        for c in range(3):
            U3[c, q(-1) : q(R + 1), PAD + C - n, :] += LX[1, 3 * n + c]
            U3[c, q(-1) : q(R + 1), PAD - 1 + n, :] += LX[0, 3 * n + c]

    @pl.when(j < nj - 1)
    def _():
        for c in range(3):
            for n in range(3):
                U3[c, q(R - 2 + n), band, :] += LR[1, c, n, band, :]

    @pl.when(j > 0)
    def _():
        for c in range(3):
            for n in range(3):
                U3[c, q(-1 + n), band, :] += LR[0, c, n, band, :]

    for n, (di, dj) in enumerate(corners):
        def add_corner(n=n, di=di, dj=dj):
            r0, c0 = (R if dj < 0 else -1), PAD + (C if di < 0 else -1)
            for m, (a, b) in enumerate(near_cells(di, dj)):
                for c in range(3):
                    at = c0 + di * b
                    U3[c, q(r0 + dj * a), at : at + 1, :] += LD[n, 3 * m + c : 3 * m + c + 1]
        pl.when(inside(-dj))(add_corner)

    for r in range(-1, R + 1):
        for c in range(3):
            x = EX[c, r // 2 + 1, lo:hi, :]
            xn = [
                EX[c, r // 2 + 1, lo - 1 : hi - 1, :],
                EX[c, r // 2 + 1, lo + 1 : hi + 1, :],
                EX[c, (r - 1) // 2 + 1, lo:hi, :],
                EX[c, (r + 1) // 2 + 1, lo:hi, :],
                pltpu.roll(x, 1, 1),
                pltpu.roll(x, LAT - 1, 1),
            ]
            t = U3[c, q(r), lo:hi, :] + 0.2 * x
            for k in range(6):
                t = t + WT[k, r + 1, lo:hi, :] * xn[k]
            U4[c, q(r), lo:hi, :] = t

    for r in range(R):
        for c in range(3):
            x, t = change(U4, c, r)
            out_ref[c, r] = x + t
    for item in round0 + coarse_visc + coarse_res:
        item.leave()


def deliver(tn_ref, out_ref, tn_hbm, out_hbm, sems):
    copies = [pltpu.make_async_copy(tn_ref, tn_hbm, sems.at[0]), pltpu.make_async_copy(out_ref, out_hbm, sems.at[1])]
    for item in copies:
        item.start()
    for item in copies:
        item.wait()


def solution(mesh):
    ni, nj = mesh.shape["lon"], mesh.shape["rad"]

    def local(adjoint_temp, viscosity, velocity, misfit_force, adjoint_guess):
        R, C, LAT = adjoint_temp.shape
        half, cols, wide = R // 4, C // 2, C + 2 * PAD
        f32 = jnp.float32
        frame = lambda n, rows: pltpu.VMEM((n, rows, wide, LAT), f32)
        block = lambda *dims: pltpu.VMEM(dims + (C, LAT), f32)
        copies = 18 + 6 * (2 * nj - 1)
        deep = R + 2 * DEEP
        vmem, place = pl.BlockSpec(memory_space=pltpu.VMEM), pl.BlockSpec(memory_space=pl.ANY)
        P8 = half * nj
        results = pl.pallas_call(
            functools.partial(kernel, ni, nj),
            out_shape=(
                pltpu.VMEM(adjoint_temp.shape, f32),
                pltpu.VMEM(adjoint_guess.shape, f32),
            ),
            in_specs=[place] * 5,
            out_specs=(vmem, vmem),
            scratch_shapes=[
                block(3, R), block(3, R), pltpu.SemaphoreType.DMA((5,)),
                frame(5, deep), frame(3, deep), frame(3, deep), frame(3, deep), frame(3, deep),
                frame(6, R + 2), frame(3, R + 2), pltpu.VMEM((R + 2, wide, LAT), f32), pltpu.VMEM((R + 2, wide, LAT), f32),
                pltpu.VMEM((3, 2 * half + 2, C + PAD, LAT), f32), block(2 * half),
                block(3, half + 1), pltpu.VMEM((1, half, cols, LAT), f32),
                block(nj + 2, 3, half + 1), block(nj + 2, 3, half + 1), block(nj + 2, 3, half + 1),
                frame(1, P8 + 2), block(7, P8), block(3, P8),
                frame(3, P8 + 2), frame(3, P8 + 2), frame(3, 2 * half + 2),
                pltpu.VMEM((2, 7, R, LAT), f32), pltpu.VMEM((2, 7, R, LAT), f32),
                pltpu.VMEM((4, 3, LAT), f32), pltpu.VMEM((4, 3, LAT), f32),
                pltpu.VMEM((2, 9, R + 2, LAT), f32), pltpu.VMEM((2, 9, R + 2, LAT), f32),
                pltpu.VMEM((2, 3, 3, wide, LAT), f32),
                pltpu.VMEM((4, 15, LAT), f32), pltpu.VMEM((4, 15, LAT), f32),
                pltpu.SemaphoreType.DMA((copies,)), pltpu.SemaphoreType.DMA((copies,)),
            ],
            compiler_params=pltpu.CompilerParams(collective_id=0, has_side_effects=True),
        )(adjoint_temp, viscosity, velocity, misfit_force, adjoint_guess)
        return pl.pallas_call(
            deliver,
            out_shape=(jax.ShapeDtypeStruct(adjoint_temp.shape, f32), jax.ShapeDtypeStruct(adjoint_guess.shape, f32)),
            in_specs=[vmem] * 2,
            out_specs=(place, place),
            scratch_shapes=[pltpu.SemaphoreType.DMA((2,))],
        )(*[pltpu.with_memory_space_constraint(item, pltpu.VMEM) for item in results])

    flat = P("rad", "lon", None)
    full = P(None, "rad", "lon", None)
    return jax.shard_map(local, mesh=mesh, in_specs=(flat, flat, full, full, full), out_specs=(flat, full), check_vma=False)
```

```python
import functools

import jax
import jax.numpy as jnp
from jax import lax
from jax.experimental import pallas as pl
from jax.experimental.pallas import tpu as pltpu
from jax.sharding import PartitionSpec as P

NU = 2
NC = 8
PAD = 8
DEEP = 3
MESH = pl.DeviceIdType.MESH


def kernel(ni, nj, temp_hbm, visc_hbm, vel_hbm, mis_hbm, guess_hbm, tn_ref, out_ref,
           vel_ref, mis_ref, local,
           W0, U1, U2, U3, U4, WT, B, D, INV, WF, RS, RV, CP, CV, GO, GW, GE, LV, CG, CW, CB, EA, EB, EX,
           S0, L0, SC, LC, SX, LX, LR, SD, LD, send, recv):
    R, C, LAT = temp_hbm.shape
    half = R // 4
    cols = C // 2
    strip = PAD
    rows = 2 * half
    i = lax.axis_index("lon")
    j = lax.axis_index("rad")
    west, east = lax.rem(i + ni - 1, ni), lax.rem(i + 1, ni)

    q = lambda r: r + DEEP
    mid = pl.ds(PAD, C)
    inner = pl.ds(DEEP, R)
    loads = [
        pltpu.make_async_copy(visc_hbm, W0.at[4, inner, mid], local.at[0]),
        pltpu.make_async_copy(temp_hbm, W0.at[3, inner, mid], local.at[1]),
        pltpu.make_async_copy(guess_hbm, W0.at[0:3, inner, mid], local.at[2]),
        pltpu.make_async_copy(vel_hbm, vel_ref, local.at[3]),
        pltpu.make_async_copy(mis_hbm, mis_ref, local.at[4]),
    ]
    for item in loads:
        item.start()

    barrier = pltpu.get_barrier_semaphore()
    for d in range(nj):
        other = lax.rem(j + d, nj)
        for lon in (west, east) if d == 0 else (west, east, i):
            pl.semaphore_signal(barrier, inc=1, device_id={"lon": lon, "rad": other}, device_id_type=MESH)

    lo, hi = PAD // 2, C + PAD + PAD // 2
    span = hi - lo
    lane_all = lax.broadcasted_iota(jnp.int32, (C + 2 * PAD, LAT), 1)
    lane = lane_all[:span]
    first, last = lane == 0, lane == LAT - 1
    parity = lax.rem(lane_all, 2)
    even = parity == 0

    edges = (pl.ds(0, PAD), pl.ds(PAD + C, PAD))
    for edge in edges:
        W0[4, :, edge, :] = jnp.ones_like(W0[4, :, edge, :])
        for buf in (B, U1, U2):
            buf[:, :, edge, :] = jnp.zeros_like(buf[:, :, edge, :])
    for c in range(3):
        for r in (0, R + 1):
            B[c, r, mid, :] = jnp.zeros((C, LAT), jnp.float32)
        for r in (-2, -1, R, R + 1):
            U1[c, q(r), mid, :] = jnp.zeros((C, LAT), jnp.float32)
        for r in (-2, R + 1):
            U2[c, q(r), mid, :] = jnp.zeros((C, LAT), jnp.float32)
    packed = half * nj
    for buf in (EA, EB):
        buf[...] = jnp.zeros_like(buf)

    def halves(a, b):
        a = a + pltpu.roll(a, LAT - 1, 1)
        b = b + pltpu.roll(b, 1, 1)
        return 0.125 * jnp.where(even[: a.shape[0]], a, b)

    def under(cond, action):
        if cond is None:
            action()
        else:
            pl.when(cond)(action)

    def copy(slot, src, dst, lon, rad):
        return pltpu.make_async_remote_copy(
            src_ref=src, dst_ref=dst, send_sem=send.at[slot], recv_sem=recv.at[slot],
            device_id={"lon": lon, "rad": rad}, device_id_type=MESH)

    class Bundle:
        def __init__(self, to, came, items):
            self.to, self.came, self.items = to, came, items

        def each(self, cond, act):
            def action():
                for item in self.items:
                    act(item)
            under(cond, action)

        def start(self):
            self.each(self.to, lambda item: item.start())

        def arrive(self):
            self.each(self.came, lambda item: item.wait_recv())

        def leave(self):
            self.each(self.to, lambda item: item.wait_send())

    inside = lambda d: (None if d == 0 else (j + d >= 0) & (j + d < nj))
    corners = [(di, dj) for di in (-1, 1) for dj in (-1, 1)]
    at_lon = {-1: west, 0: i, 1: east}

    loads[0].wait()
    for p in range(rows):
        RV[p] = W0[4, q(2 * p), mid, :] + W0[4, q(2 * p + 1), mid, :]
    for r in range(half):
        a = RV[r, pl.ds(0, cols, 2), :] + RV[r, pl.ds(1, cols, 2), :]
        b = RV[r + half, pl.ds(0, cols, 2), :] + RV[r + half, pl.ds(1, cols, 2), :]
        CV[0, r] = halves(a, b)
    for n in range(3):
        S0[0, 4 + n] = W0[4, inner, PAD + n, :]
        S0[1, 4 + n] = W0[4, inner, PAD + C - 1 - n, :]
    for n, (di, dj) in enumerate(corners):
        r0, c0 = (0 if dj < 0 else R - 1), PAD + (0 if di < 0 else C - 1)
        SC[n, 0:1] = W0[4, q(r0), c0 : c0 + 1, :]
        SC[n, 1:2] = W0[4, q(r0), c0 - di : c0 - di + 1, :]
        SC[n, 2:3] = W0[4, q(r0 - dj), c0 : c0 + 1, :]
    loads[1].wait()
    loads[2].wait()
    for c in range(4):
        S0[0, c] = W0[c, inner, PAD, :]
        S0[1, c] = W0[c, inner, PAD + C - 1, :]
    pl.semaphore_wait(barrier, 3 * nj - 1)

    round0 = [Bundle(None, None, [copy(0, S0.at[0], L0.at[1], west, j), copy(1, S0.at[1], L0.at[0], east, j)])]
    diagonal = lambda slot, src, dst, dj: [
        copy(slot + n, src.at[n], dst.at[n], at_lon[di], j + dj) for n, (di, d) in enumerate(corners) if d == dj]
    round0.append(Bundle(inside(-1), inside(1), [
        copy(2, W0.at[:, q(0), mid], W0.at[:, q(R), mid], i, j - 1),
        copy(3, W0.at[4, pl.ds(q(1), 2), mid], W0.at[4, pl.ds(q(R + 1), 2), mid], i, j - 1),
    ] + diagonal(6, SC, LC, -1)))
    round0.append(Bundle(inside(1), inside(-1), [
        copy(4, W0.at[:, q(R - 1), mid], W0.at[:, q(-1), mid], i, j + 1),
        copy(5, W0.at[4, pl.ds(q(R - 3), 2), mid], W0.at[4, pl.ds(q(-3), 2), mid], i, j + 1),
    ] + diagonal(6, SC, LC, 1)))
    for item in round0:
        item.start()

    other_core = j + 1 - 2 * lax.rem(j, 2)
    alike = [lax.rem(j + 2 * k, nj) for k in range(1, nj // 2)]
    legs = 3 * nj - 1

    def relay(slot, src, dst):
        route = [(di, j, src[di], dst[di](j)) for di in (-1, 1)]
        route += [(di, rad, src[di], dst[di](j)) for rad in alike for di in (-1, 1, 0)]
        route += [(0, other_core, src[0], dst[0](j))]
        direct = Bundle(None, None, [copy(slot + n, a, b, at_lon[di], rad) for n, (di, rad, a, b) in enumerate(route)])
        slot = slot + len(route)
        hand = [dst[di](j) for di in (-1, 1)] + [dst[di](rad) for rad in alike for di in (-1, 1, 0)]
        onward = Bundle(None, None, [copy(slot + n, ref, ref, i, other_core) for n, ref in enumerate(hand)])
        direct.start()
        return direct, onward

    def visc_place(start, width):
        return lambda rad: LV.at[rad, :, pl.ds(start, width)]

    deep = NC + 1
    visc_direct, visc_onward = relay(10, {
        -1: CV.at[0, :, pl.ds(0, deep)], 0: CV.at[0], 1: CV.at[0, :, pl.ds(cols - deep, deep)],
    }, {
        -1: visc_place(2 * strip + cols, deep), 0: visc_place(2 * strip, cols), 1: visc_place(2 * strip - deep, deep),
    })
    for r in range(half):
        LV[j, r, 2 * strip : 2 * strip + cols, :] = CV[0, r]
    loads[3].wait()
    loads[4].wait()

    for item in round0:
        item.arrive()
    for c in range(4):
        W0[c, inner, PAD - 1, :] = L0[0, c]
        W0[c, inner, PAD + C, :] = L0[1, c]
    for n in range(3):
        W0[4, inner, PAD - 1 - n, :] = L0[0, 4 + n]
        W0[4, inner, PAD + C + n, :] = L0[1, 4 + n]
    for n, (di, dj) in enumerate(corners):
        rr, cc = (R if dj < 0 else -1), PAD + (C if di < 0 else -1)
        def place_corner(n=n, di=di, dj=dj, rr=rr, cc=cc):
            W0[4, q(rr), cc : cc + 1, :] = LC[n, 0:1]
            W0[4, q(rr), cc - di : cc - di + 1, :] = LC[n, 1:2]
            W0[4, q(rr - dj), cc : cc + 1, :] = LC[n, 2:3]
        pl.when(inside(-dj))(place_corner)

    @pl.when(j == 0)
    def _():
        W0[:, q(-1)] = jnp.zeros_like(W0[:, q(-1)])
        W0[4, q(-3) : q(-1)] = jnp.ones_like(W0[4, q(-3) : q(-1)])

    @pl.when(j == nj - 1)
    def _():
        W0[:, q(R)] = jnp.zeros_like(W0[:, q(R)])
        W0[4, q(R + 1) : q(R + 3)] = jnp.ones_like(W0[4, q(R + 1) : q(R + 3)])

    def near(buf, c, r, lo=PAD, width=C):
        hi = lo + width
        x = buf[c, q(r), lo:hi, :]
        return x, [
            buf[c, q(r), lo - 1 : hi - 1, :],
            buf[c, q(r), lo + 1 : hi + 1, :],
            buf[c, q(r - 1), lo:hi, :],
            buf[c, q(r + 1), lo:hi, :],
            pltpu.roll(x, 1, 1),
            pltpu.roll(x, LAT - 1, 1),
        ]

    def faces(r):
        v, vn = near(W0, 4, r, lo, span)
        vn[4] = jnp.where(first, 0.0, vn[4])
        vn[5] = jnp.where(last, 0.0, vn[5])
        coefs = [(v + item) * 0.5 for item in vn]
        diag = coefs[0] + coefs[1] + coefs[2] + coefs[3] + coefs[4] + coefs[5]
        return coefs, diag, 0.8 / diag

    for r in range(-1, R + 1):
        coefs, diag, inv = faces(r)
        coefs[4] = jnp.where(first, 0.0, coefs[4])
        coefs[5] = jnp.where(last, 0.0, coefs[5])
        for k in range(6):
            WT[k, r + 1, lo:hi, :] = coefs[k] * inv
        D[r + 1, lo:hi, :] = diag * 1.25
        INV[r + 1, lo:hi, :] = inv
    for n, (r, k) in enumerate(((-2, 3), (R + 1, 2))):
        coefs, diag, inv = faces(r)
        WF[0, n, lo:hi, :] = coefs[k] * inv
        WF[1, n, lo:hi, :] = coefs[k]

    for r in range(R):
        inv = INV[r + 1, mid, :]
        t, tn = near(W0, 3, r)
        tn[4] = jnp.where(first[:C], 0.0, tn[4])
        tn[5] = jnp.where(last[:C], 0.0, tn[5])
        advect = vel_ref[0, r] * (tn[3] - tn[2]) + vel_ref[1, r] * (tn[1] - tn[0]) + vel_ref[2, r] * (tn[5] - tn[4])
        spread_t = tn[0] + tn[1] + tn[2] + tn[3] + tn[4] + tn[5] - 6.0 * t
        t_next = t + 0.125 * advect + 0.1 * spread_t
        tn_ref[r] = t_next
        B[0, r + 1, mid, :] = (mis_ref[0, r] + t_next) * inv
        B[1, r + 1, mid, :] = mis_ref[1, r] * inv
        B[2, r + 1, mid, :] = mis_ref[2, r] * inv

    @pl.when(j == 0)
    def _():
        WT[2, 1] = jnp.zeros_like(WT[2, 1])
        WT[:, 0] = jnp.zeros_like(WT[:, 0])

    @pl.when(j == nj - 1)
    def _():
        WT[3, R] = jnp.zeros_like(WT[3, R])
        WT[:, R + 1] = jnp.zeros_like(WT[:, R + 1])

    def change(buf, c, r, lo=PAD, width=C):
        x, xn = near(buf, c, r, lo, width)
        t = B[c, r + 1, lo : lo + width, :] - 0.8 * x
        for k in range(6):
            t = t + WT[k, r + 1, lo : lo + width, :] * xn[k]
        return x, t

    for r in range(R):
        for c in range(3):
            x, t = change(W0, c, r)
            U1[c, q(r), mid, :] = x + t

    def residual(c, r):
        x, t = change(U2, c, r, lo, span)
        U3[c, q(r), lo:hi, :] = x + t
        return D[r + 1, lo:hi, :] * t

    def part(c, slot):
        width = NC + 1
        place = lambda buf, start, size: lambda rad: buf.at[rad + 1, c, :, pl.ds(start, size)]
        return relay(slot, {
            -1: CP.at[c, :, pl.ds(strip - 1, width)],
            0: CP.at[c, :, pl.ds(strip - 1, cols + 2)],
            1: CP.at[c, :, pl.ds(strip + cols - NC, width)],
        }, {
            -1: place(GE, strip - 1 + cols, width),
            0: place(GO, strip - 1, cols + 2),
            1: place(GW, strip - NC, width),
        })

    wide_c = span // 2
    slot = 10 + legs
    coarse_res = []
    for c in range(3):
        U2[c, q(-1), mid, :] = WT[3, 0, mid, :] * U1[c, q(0), mid, :]
        U2[c, q(R), mid, :] = WT[2, R + 1, mid, :] * U1[c, q(R - 1), mid, :]
        for r in range(R):
            x, t = change(U1, c, r, lo, span)
            U2[c, q(r), lo:hi, :] = x + t
        for r, k, p in ((-2, 3, 0), (R + 1, 2, rows + 1)):
            other = -1 if r < 0 else R
            x = U2[c, q(other), lo:hi, :]
            U3[c, q(r), lo:hi, :] = WF[0, int(p > 0), lo:hi, :] * x
            RS[c, p] = WF[1, int(p > 0), lo:hi, :] * x + residual(c, other)
        for p in range(rows):
            RS[c, p + 1] = residual(c, 2 * p) + residual(c, 2 * p + 1)
        pair = lambda p: RS[c, p + 1, pl.ds(0, wide_c, 2), :] + RS[c, p + 1, pl.ds(1, wide_c, 2), :]
        for r, a, b in [(r, r, r + half) for r in range(half)] + [(half, rows, -1)]:
            CP[c, r, strip - 2 : strip - 2 + wide_c, :] = halves(pair(a), pair(b))
        coarse_res.append(part(c, slot))
        slot = slot + legs
        if c == 0:
            visc_direct.arrive()
            visc_onward.start()

    near_cells = [(0, 1), (0, 2), (1, 1), (1, 0), (2, 0)]
    band = pl.ds(PAD - 1, C + 2)
    for n, (di, dj) in enumerate(corners):
        r0, c0 = (0 if dj < 0 else R - 1), PAD + (0 if di < 0 else C - 1)
        for m, (a, b) in enumerate(near_cells):
            for c in range(3):
                at = c0 + di * b
                SD[n, 3 * m + c : 3 * m + c + 1] = U3[c, q(r0 + dj * a), at : at + 1, :]
    fine = []
    for c in range(3):
        for n in range(3):
            SX[0, c, n] = U3[c, q(-1) : q(R + 1), PAD - n, :]
            SX[1, c, n] = U3[c, q(-1) : q(R + 1), PAD + C - 1 + n, :]
        group = [
            Bundle(None, None, [copy(slot, SX.at[0, c], LX.at[1, c], west, j), copy(slot + 1, SX.at[1, c], LX.at[0, c], east, j)]),
            Bundle(inside(-1), inside(1), [
                copy(slot + 2, U3.at[c, pl.ds(q(-2), 3), band], LR.at[1, c, :, band], i, j - 1),
            ] + (diagonal(slot + 4, SD, LD, -1) if c == 0 else [])),
            Bundle(inside(1), inside(-1), [
                copy(slot + 3, U3.at[c, pl.ds(q(R - 1), 3), band], LR.at[0, c, :, band], i, j + 1),
            ] + (diagonal(slot + 4, SD, LD, 1) if c == 0 else [])),
        ]
        slot = slot + (8 if c == 0 else 4)
        for item in group:
            item.start()
        fine.append(group)

    visc_onward.arrive()

    lane_c = lane[:C]

    def repack(get, p):
        s, r = p // rows, p % rows
        a, b = get(s, r % half), get(s + nj // 2, r % half)
        if r >= half:
            a = pltpu.roll(a, LAT - 1, 1)
        else:
            b = pltpu.roll(b, 1, 1)
        return jnp.where(even[: a.shape[0]], a, b)

    def coarse_near(buf, c, p, lo=PAD, width=C):
        part = even[:width]
        block = lambda place, off=0: buf[c, place, lo + off : lo + off + width, :]
        x = block(p)
        below = block(p - 1) if p > 0 else jnp.where(part, 0.0, pltpu.roll(block(packed - 1), 1, 1))
        above = block(p + 1) if p < packed - 1 else jnp.where(part, pltpu.roll(block(0), LAT - 1, 1), 0.0)
        return x, [block(p, -1), block(p, 1), below, above, pltpu.roll(x, 2, 1), pltpu.roll(x, LAT - 2, 1)]

    for p in range(packed):
        CG[0, p] = repack(lambda s, r: LV[s, r], p)
    for p in range(packed):
        v, vn = coarse_near(CG, 0, p)
        vn[4] = jnp.where(lane_c < 2, 0.0, vn[4])
        vn[5] = jnp.where(lane_c >= LAT - 2, 0.0, vn[5])
        coefs = [(v + item) * 0.5 for item in vn]
        diag = coefs[0] + coefs[1] + coefs[2] + coefs[3] + coefs[4] + coefs[5]
        inv = 0.8 / diag
        coefs[4] = jnp.where(lane_c < 2, 0.0, coefs[4])
        coefs[5] = jnp.where(lane_c >= LAT - 2, 0.0, coefs[5])
        for k in range(6):
            CW[k, p] = coefs[k] * inv
        CW[6, p] = 4.0 * inv

    for r in range(half + 1):
        for c in range(3):
            GO[j + 1, c, r] = CP[c, r]

    col = lax.broadcasted_iota(jnp.int32, (C, LAT), 0)
    own = (col >= strip - 1) & (col <= strip + cols)
    before, after = col <= strip, col >= strip + cols - 1

    def total(s, c, p):
        x = jnp.where(own, GO[s + 1, c, p], 0.0)
        return x + jnp.where(before, GW[s + 1, c, p], 0.0) + jnp.where(after, GE[s + 1, c, p], 0.0)

    even_c = even[:C]

    def coarse_part(s, c, r):
        b = total(s, c, r)
        if r == 0 and s > 0:
            b = b + jnp.where(even_c, total(s - 1, c, half), 0.0)
        if r == half - 1 and s < nj - 1:
            b = b + jnp.where(even_c, 0.0, total(s + 1, c, half))
        return b

    def coarse_sweep(src, dst, rim):
        near_rim = 2 * rim <= PAD and cols % 8 == 0
        lo = 2 * strip - PAD // 2 if near_rim else PAD
        width = cols + PAD if near_rim else C
        for p in range(packed):
            for c in range(3):
                x, xn = coarse_near(src, c, p, lo, width)
                t = CB[c, p, lo - PAD : lo - PAD + width, :] + 0.2 * x
                for k in range(6):
                    t = t + CW[k, p, lo - PAD : lo - PAD + width, :] * xn[k]
                dst[c, p, lo : lo + width, :] = t

    def hand_on(c):
        coarse_res[c][0].arrive()
        coarse_res[c][1].start()

    for c in range(3):
        hand_on(c)
    for c in range(3):
        coarse_res[c][1].arrive()
    for p in range(packed):
        for c in range(3):
            b = repack(lambda s, r: coarse_part(s, c, r), p) * CW[6, p]
            CB[c, p] = b
            EA[c, p, PAD : PAD + C, :] = b
    src, dst = EA, EB
    for number in range(NC - 1):
        coarse_sweep(src, dst, NC - 1 - number)
        src, dst = dst, src
    wide = EX.shape[2] // 2
    start = 2 * strip - PAD // 2
    for m in range(-1, rows + 1):
        at = rows * j + m
        upper = (at >= packed).astype(jnp.int32)
        valid = parity[:wide] == upper
        for c in range(3):
            x = src[c, lax.rem(at + packed, packed), start : start + wide, :]
            other = jnp.where(upper == 1, pltpu.roll(x, LAT - 1, 1), pltpu.roll(x, 1, 1))
            x = jnp.where(valid, x, other)
            EX[c, m + 1, pl.ds(0, wide, 2), :] = x
            EX[c, m + 1, pl.ds(1, wide, 2), :] = x

    def from_above(c):
        for n in range(3):
            U3[c, q(R - 2 + n), band, :] += LR[1, c, n, band, :]

    def from_below(c):
        for n in range(3):
            U3[c, q(-1 + n), band, :] += LR[0, c, n, band, :]

    def add_corner(c, n, di, dj):
        r0, c0 = (R if dj < 0 else -1), PAD + (C if di < 0 else -1)
        for m, (a, b) in enumerate(near_cells):
            at = c0 + di * b
            U3[c, q(r0 + dj * a), at : at + 1, :] += LD[n, 3 * m + c : 3 * m + c + 1]

    for c in range(3):
        for item in fine[c]:
            item.arrive()
            item.leave()
        for n in range(3):
            U3[c, q(-1) : q(R + 1), PAD + C - n, :] += LX[1, c, n]
            U3[c, q(-1) : q(R + 1), PAD - 1 + n, :] += LX[0, c, n]

        @pl.when(j < nj - 1)
        def _():
            from_above(c)
            for n, (di, dj) in enumerate(corners):
                if dj < 0:
                    add_corner(c, n, di, dj)

        @pl.when(j > 0)
        def _():
            from_below(c)
            for n, (di, dj) in enumerate(corners):
                if dj > 0:
                    add_corner(c, n, di, dj)

    for r in range(-1, R + 1):
        for c in range(3):
            x = EX[c, r // 2 + 1, lo:hi, :]
            xn = [
                EX[c, r // 2 + 1, lo - 1 : hi - 1, :],
                EX[c, r // 2 + 1, lo + 1 : hi + 1, :],
                EX[c, (r - 1) // 2 + 1, lo:hi, :],
                EX[c, (r + 1) // 2 + 1, lo:hi, :],
                pltpu.roll(x, 1, 1),
                pltpu.roll(x, LAT - 1, 1),
            ]
            t = U3[c, q(r), lo:hi, :] + 0.2 * x
            for k in range(6):
                t = t + WT[k, r + 1, lo:hi, :] * xn[k]
            U4[c, q(r), lo:hi, :] = t
    for r in range(R):
        for c in range(3):
            x, t = change(U4, c, r)
            out_ref[c, r] = x + t
    for item in round0:
        item.leave()
    for pair in [(visc_direct, visc_onward)] + coarse_res:
        for item in pair:
            item.leave()


def deliver(tn_ref, out_ref, tn_hbm, out_hbm, sems):
    copies = [pltpu.make_async_copy(tn_ref, tn_hbm, sems.at[0]), pltpu.make_async_copy(out_ref, out_hbm, sems.at[1])]
    for item in copies:
        item.start()
    for item in copies:
        item.wait()


def solution(mesh):
    ni, nj = mesh.shape["lon"], mesh.shape["rad"]

    def local(adjoint_temp, viscosity, velocity, misfit_force, adjoint_guess):
        R, C, LAT = adjoint_temp.shape
        half, cols, wide = R // 4, C // 2, C + 2 * PAD
        f32 = jnp.float32
        frame = lambda n, rows: pltpu.VMEM((n, rows, wide, LAT), f32)
        block = lambda *dims: pltpu.VMEM(dims + (C, LAT), f32)
        copies = 26 + 4 * (3 * nj - 1)
        deep = R + 2 * DEEP
        vmem, place = pl.BlockSpec(memory_space=pltpu.VMEM), pl.BlockSpec(memory_space=pl.ANY)
        P8 = half * nj
        results = pl.pallas_call(
            functools.partial(kernel, ni, nj),
            out_shape=(
                pltpu.VMEM(adjoint_temp.shape, f32),
                pltpu.VMEM(adjoint_guess.shape, f32),
            ),
            in_specs=[place] * 5,
            out_specs=(vmem, vmem),
            scratch_shapes=[
                block(3, R), block(3, R), pltpu.SemaphoreType.DMA((5,)),
                frame(5, deep), frame(3, deep), frame(3, deep), frame(3, deep), frame(3, deep),
                frame(6, R + 2), frame(3, R + 2), pltpu.VMEM((R + 2, wide, LAT), f32), pltpu.VMEM((R + 2, wide, LAT), f32), frame(2, 2),
                pltpu.VMEM((3, 2 * half + 2, C + PAD, LAT), f32), block(2 * half),
                block(3, half + 1), pltpu.VMEM((1, half, cols, LAT), f32),
                block(nj + 2, 3, half + 1), block(nj + 2, 3, half + 1), block(nj + 2, 3, half + 1),
                pltpu.VMEM((nj, half, wide, LAT), f32), frame(1, P8), block(7, P8), block(3, P8),
                frame(3, P8), frame(3, P8), frame(3, 2 * half + 2),
                pltpu.VMEM((2, 7, R, LAT), f32), pltpu.VMEM((2, 7, R, LAT), f32),
                pltpu.VMEM((4, 3, LAT), f32), pltpu.VMEM((4, 3, LAT), f32),
                pltpu.VMEM((2, 3, 3, R + 2, LAT), f32), pltpu.VMEM((2, 3, 3, R + 2, LAT), f32),
                pltpu.VMEM((2, 3, 3, wide, LAT), f32),
                pltpu.VMEM((4, 15, LAT), f32), pltpu.VMEM((4, 15, LAT), f32),
                pltpu.SemaphoreType.DMA((copies,)), pltpu.SemaphoreType.DMA((copies,)),
            ],
            compiler_params=pltpu.CompilerParams(collective_id=0, has_side_effects=True),
        )(adjoint_temp, viscosity, velocity, misfit_force, adjoint_guess)
        return pl.pallas_call(
            deliver,
            out_shape=(jax.ShapeDtypeStruct(adjoint_temp.shape, f32), jax.ShapeDtypeStruct(adjoint_guess.shape, f32)),
            in_specs=[vmem] * 2,
            out_specs=(place, place),
            scratch_shapes=[pltpu.SemaphoreType.DMA((2,))],
        )(*[pltpu.with_memory_space_constraint(item, pltpu.VMEM) for item in results])

    flat = P("rad", "lon", None)
    full = P(None, "rad", "lon", None)
    return jax.shard_map(local, mesh=mesh, in_specs=(flat, flat, full, full, full), out_specs=(flat, full), check_vma=False)
```

```python
import functools

import jax
import jax.numpy as jnp
from jax import lax
from jax.experimental import pallas as pl
from jax.experimental.pallas import tpu as pltpu
from jax.sharding import PartitionSpec as P

NU = 2
NC = 8
PAD = 8
DEEP = 3
MESH = pl.DeviceIdType.MESH


def kernel(ni, nj, temp_hbm, visc_hbm, vel_hbm, mis_hbm, guess_hbm, tn_ref, out_ref,
           vel_ref, mis_ref, local,
           W0, U1, U2, U3, U4, WT, B, D, INV, WF, RS, RV, CP, CV, GO, GW, GE, LV, CG, CW, CB, EA, EB, EX,
           S0, L0, SC, LC, SX, LX, LR, SD, LD, send, recv):
    R, C, LAT = temp_hbm.shape
    half = R // 4
    cols = C // 2
    strip = PAD
    rows = 2 * half
    i = lax.axis_index("lon")
    j = lax.axis_index("rad")
    west, east = lax.rem(i + ni - 1, ni), lax.rem(i + 1, ni)

    q = lambda r: r + DEEP
    mid = pl.ds(PAD, C)
    inner = pl.ds(DEEP, R)
    loads = [
        pltpu.make_async_copy(visc_hbm, W0.at[4, inner, mid], local.at[0]),
        pltpu.make_async_copy(temp_hbm, W0.at[3, inner, mid], local.at[1]),
        pltpu.make_async_copy(guess_hbm, W0.at[0:3, inner, mid], local.at[2]),
        pltpu.make_async_copy(vel_hbm, vel_ref, local.at[3]),
        pltpu.make_async_copy(mis_hbm, mis_ref, local.at[4]),
    ]
    for item in loads[:3]:
        item.start()

    barrier = pltpu.get_barrier_semaphore()
    for d in range(nj):
        other = lax.rem(j + d, nj)
        for lon in (west, east) if d == 0 else (west, east, i):
            pl.semaphore_signal(barrier, inc=1, device_id={"lon": lon, "rad": other}, device_id_type=MESH)

    lo, hi = PAD // 2, C + PAD + PAD // 2
    span = hi - lo
    lane_all = lax.broadcasted_iota(jnp.int32, (C + 2 * PAD, LAT), 1)
    lane = lane_all[:span]
    first, last = lane == 0, lane == LAT - 1
    parity = lax.rem(lane_all, 2)
    even = parity == 0

    edges = (pl.ds(0, PAD), pl.ds(PAD + C, PAD))
    for edge in edges:
        W0[4, :, edge, :] = jnp.ones_like(W0[4, :, edge, :])
        for buf in (B, U1, U2):
            buf[:, :, edge, :] = jnp.zeros_like(buf[:, :, edge, :])
    for c in range(3):
        for r in (0, R + 1):
            B[c, r, mid, :] = jnp.zeros((C, LAT), jnp.float32)
        for r in (-2, -1, R, R + 1):
            U1[c, q(r), mid, :] = jnp.zeros((C, LAT), jnp.float32)
        for r in (-2, R + 1):
            U2[c, q(r), mid, :] = jnp.zeros((C, LAT), jnp.float32)
    packed = half * nj
    for buf in (EA, EB):
        buf[...] = jnp.zeros_like(buf)

    def halves(a, b):
        a = a + pltpu.roll(a, LAT - 1, 1)
        b = b + pltpu.roll(b, 1, 1)
        return 0.125 * jnp.where(even[: a.shape[0]], a, b)

    def under(cond, action):
        if cond is None:
            action()
        else:
            pl.when(cond)(action)

    def copy(slot, src, dst, lon, rad):
        return pltpu.make_async_remote_copy(
            src_ref=src, dst_ref=dst, send_sem=send.at[slot], recv_sem=recv.at[slot],
            device_id={"lon": lon, "rad": rad}, device_id_type=MESH)

    class Bundle:
        def __init__(self, to, came, items):
            self.to, self.came, self.items = to, came, items

        def each(self, cond, act):
            def action():
                for item in self.items:
                    act(item)
            under(cond, action)

        def start(self):
            self.each(self.to, lambda item: item.start())

        def arrive(self):
            self.each(self.came, lambda item: item.wait_recv())

        def leave(self):
            self.each(self.to, lambda item: item.wait_send())

    inside = lambda d: (None if d == 0 else (j + d >= 0) & (j + d < nj))
    corners = [(di, dj) for di in (-1, 1) for dj in (-1, 1)]
    at_lon = {-1: west, 0: i, 1: east}

    loads[0].wait()
    for p in range(rows):
        RV[p] = W0[4, q(2 * p), mid, :] + W0[4, q(2 * p + 1), mid, :]
    for r in range(half):
        a = RV[r, pl.ds(0, cols, 2), :] + RV[r, pl.ds(1, cols, 2), :]
        b = RV[r + half, pl.ds(0, cols, 2), :] + RV[r + half, pl.ds(1, cols, 2), :]
        CV[0, r] = halves(a, b)
    for n in range(3):
        S0[0, 4 + n] = W0[4, inner, PAD + n, :]
        S0[1, 4 + n] = W0[4, inner, PAD + C - 1 - n, :]
    for n, (di, dj) in enumerate(corners):
        r0, c0 = (0 if dj < 0 else R - 1), PAD + (0 if di < 0 else C - 1)
        SC[n, 0:1] = W0[4, q(r0), c0 : c0 + 1, :]
        SC[n, 1:2] = W0[4, q(r0), c0 - di : c0 - di + 1, :]
        SC[n, 2:3] = W0[4, q(r0 - dj), c0 : c0 + 1, :]
    loads[1].wait()
    loads[2].wait()
    for c in range(4):
        S0[0, c] = W0[c, inner, PAD, :]
        S0[1, c] = W0[c, inner, PAD + C - 1, :]
    pl.semaphore_wait(barrier, 3 * nj - 1)

    round0 = [Bundle(None, None, [copy(0, S0.at[0], L0.at[1], west, j), copy(1, S0.at[1], L0.at[0], east, j)])]
    diagonal = lambda slot, src, dst, dj: [
        copy(slot + n, src.at[n], dst.at[n], at_lon[di], j + dj) for n, (di, d) in enumerate(corners) if d == dj]
    round0.append(Bundle(inside(-1), inside(1), [
        copy(2, W0.at[:, q(0), mid], W0.at[:, q(R), mid], i, j - 1),
        copy(3, W0.at[4, pl.ds(q(1), 2), mid], W0.at[4, pl.ds(q(R + 1), 2), mid], i, j - 1),
    ] + diagonal(6, SC, LC, -1)))
    round0.append(Bundle(inside(1), inside(-1), [
        copy(4, W0.at[:, q(R - 1), mid], W0.at[:, q(-1), mid], i, j + 1),
        copy(5, W0.at[4, pl.ds(q(R - 3), 2), mid], W0.at[4, pl.ds(q(-3), 2), mid], i, j + 1),
    ] + diagonal(6, SC, LC, 1)))
    for item in round0:
        item.start()
    for item in loads[3:]:
        item.start()

    other_core = j + 1 - 2 * lax.rem(j, 2)
    alike = [lax.rem(j + 2 * k, nj) for k in range(1, nj // 2)]
    legs = 3 * nj - 1

    def relay(slot, src, dst):
        route = [(di, j, src[di], dst[di](j)) for di in (-1, 1)]
        route += [(di, rad, src[di], dst[di](j)) for rad in alike for di in (-1, 1, 0)]
        route += [(0, other_core, src[0], dst[0](j))]
        direct = Bundle(None, None, [copy(slot + n, a, b, at_lon[di], rad) for n, (di, rad, a, b) in enumerate(route)])
        slot = slot + len(route)
        hand = [dst[di](j) for di in (-1, 1)] + [dst[di](rad) for rad in alike for di in (-1, 1, 0)]
        onward = Bundle(None, None, [copy(slot + n, ref, ref, i, other_core) for n, ref in enumerate(hand)])
        direct.start()
        return direct, onward

    def visc_place(start, width):
        return lambda rad: LV.at[rad, :, pl.ds(start, width)]

    deep = NC + 1
    visc_direct, visc_onward = relay(10, {
        -1: CV.at[0, :, pl.ds(0, deep)], 0: CV.at[0], 1: CV.at[0, :, pl.ds(cols - deep, deep)],
    }, {
        -1: visc_place(2 * strip + cols, deep), 0: visc_place(2 * strip, cols), 1: visc_place(2 * strip - deep, deep),
    })
    for r in range(half):
        LV[j, r, 2 * strip : 2 * strip + cols, :] = CV[0, r]
    loads[3].wait()
    loads[4].wait()

    for item in round0:
        item.arrive()
    for c in range(4):
        W0[c, inner, PAD - 1, :] = L0[0, c]
        W0[c, inner, PAD + C, :] = L0[1, c]
    for n in range(3):
        W0[4, inner, PAD - 1 - n, :] = L0[0, 4 + n]
        W0[4, inner, PAD + C + n, :] = L0[1, 4 + n]
    for n, (di, dj) in enumerate(corners):
        rr, cc = (R if dj < 0 else -1), PAD + (C if di < 0 else -1)
        def place_corner(n=n, di=di, dj=dj, rr=rr, cc=cc):
            W0[4, q(rr), cc : cc + 1, :] = LC[n, 0:1]
            W0[4, q(rr), cc - di : cc - di + 1, :] = LC[n, 1:2]
            W0[4, q(rr - dj), cc : cc + 1, :] = LC[n, 2:3]
        pl.when(inside(-dj))(place_corner)

    @pl.when(j == 0)
    def _():
        W0[:, q(-1)] = jnp.zeros_like(W0[:, q(-1)])
        W0[4, q(-3) : q(-1)] = jnp.ones_like(W0[4, q(-3) : q(-1)])

    @pl.when(j == nj - 1)
    def _():
        W0[:, q(R)] = jnp.zeros_like(W0[:, q(R)])
        W0[4, q(R + 1) : q(R + 3)] = jnp.ones_like(W0[4, q(R + 1) : q(R + 3)])

    def near(buf, c, r, lo=PAD, width=C):
        hi = lo + width
        x = buf[c, q(r), lo:hi, :]
        return x, [
            buf[c, q(r), lo - 1 : hi - 1, :],
            buf[c, q(r), lo + 1 : hi + 1, :],
            buf[c, q(r - 1), lo:hi, :],
            buf[c, q(r + 1), lo:hi, :],
            pltpu.roll(x, 1, 1),
            pltpu.roll(x, LAT - 1, 1),
        ]

    def faces(r):
        v, vn = near(W0, 4, r, lo, span)
        vn[4] = jnp.where(first, 0.0, vn[4])
        vn[5] = jnp.where(last, 0.0, vn[5])
        coefs = [(v + item) * 0.5 for item in vn]
        diag = coefs[0] + coefs[1] + coefs[2] + coefs[3] + coefs[4] + coefs[5]
        return coefs, diag, 0.8 / diag

    for r in range(-1, R + 1):
        coefs, diag, inv = faces(r)
        coefs[4] = jnp.where(first, 0.0, coefs[4])
        coefs[5] = jnp.where(last, 0.0, coefs[5])
        for k in range(6):
            WT[k, r + 1, lo:hi, :] = coefs[k] * inv
        D[r + 1, lo:hi, :] = diag * 1.25
        INV[r + 1, lo:hi, :] = inv
    for n, (r, k) in enumerate(((-2, 3), (R + 1, 2))):
        coefs, diag, inv = faces(r)
        WF[0, n, lo:hi, :] = coefs[k] * inv
        WF[1, n, lo:hi, :] = coefs[k]

    for r in range(R):
        inv = INV[r + 1, mid, :]
        t, tn = near(W0, 3, r)
        tn[4] = jnp.where(first[:C], 0.0, tn[4])
        tn[5] = jnp.where(last[:C], 0.0, tn[5])
        advect = vel_ref[0, r] * (tn[3] - tn[2]) + vel_ref[1, r] * (tn[1] - tn[0]) + vel_ref[2, r] * (tn[5] - tn[4])
        spread_t = tn[0] + tn[1] + tn[2] + tn[3] + tn[4] + tn[5] - 6.0 * t
        t_next = t + 0.125 * advect + 0.1 * spread_t
        tn_ref[r] = t_next
        B[0, r + 1, mid, :] = (mis_ref[0, r] + t_next) * inv
        B[1, r + 1, mid, :] = mis_ref[1, r] * inv
        B[2, r + 1, mid, :] = mis_ref[2, r] * inv

    @pl.when(j == 0)
    def _():
        WT[2, 1] = jnp.zeros_like(WT[2, 1])
        WT[:, 0] = jnp.zeros_like(WT[:, 0])

    @pl.when(j == nj - 1)
    def _():
        WT[3, R] = jnp.zeros_like(WT[3, R])
        WT[:, R + 1] = jnp.zeros_like(WT[:, R + 1])

    def change(buf, c, r, lo=PAD, width=C):
        x, xn = near(buf, c, r, lo, width)
        t = B[c, r + 1, lo : lo + width, :] - 0.8 * x
        for k in range(6):
            t = t + WT[k, r + 1, lo : lo + width, :] * xn[k]
        return x, t

    for r in range(R):
        for c in range(3):
            x, t = change(W0, c, r)
            U1[c, q(r), mid, :] = x + t

    def residual(c, r):
        x, t = change(U2, c, r, lo, span)
        U3[c, q(r), lo:hi, :] = x + t
        return D[r + 1, lo:hi, :] * t

    def part(c, slot):
        width = NC + 1
        place = lambda buf, start, size: lambda rad: buf.at[rad + 1, c, :, pl.ds(start, size)]
        return relay(slot, {
            -1: CP.at[c, :, pl.ds(strip - 1, width)],
            0: CP.at[c, :, pl.ds(strip - 1, cols + 2)],
            1: CP.at[c, :, pl.ds(strip + cols - NC, width)],
        }, {
            -1: place(GE, strip - 1 + cols, width),
            0: place(GO, strip - 1, cols + 2),
            1: place(GW, strip - NC, width),
        })

    wide_c = span // 2
    slot = 10 + legs
    coarse_res = []
    for c in range(3):
        U2[c, q(-1), mid, :] = WT[3, 0, mid, :] * U1[c, q(0), mid, :]
        U2[c, q(R), mid, :] = WT[2, R + 1, mid, :] * U1[c, q(R - 1), mid, :]
        for r in range(R):
            x, t = change(U1, c, r, lo, span)
            U2[c, q(r), lo:hi, :] = x + t
        for r, k, p in ((-2, 3, 0), (R + 1, 2, rows + 1)):
            other = -1 if r < 0 else R
            x = U2[c, q(other), lo:hi, :]
            U3[c, q(r), lo:hi, :] = WF[0, int(p > 0), lo:hi, :] * x
            RS[c, p] = WF[1, int(p > 0), lo:hi, :] * x + residual(c, other)
        for p in range(rows):
            RS[c, p + 1] = residual(c, 2 * p) + residual(c, 2 * p + 1)
        pair = lambda p: RS[c, p + 1, pl.ds(0, wide_c, 2), :] + RS[c, p + 1, pl.ds(1, wide_c, 2), :]
        for r, a, b in [(r, r, r + half) for r in range(half)] + [(half, rows, -1)]:
            CP[c, r, strip - 2 : strip - 2 + wide_c, :] = halves(pair(a), pair(b))
        coarse_res.append(part(c, slot))
        slot = slot + legs
        if c == 0:
            visc_direct.arrive()
            visc_onward.start()

    near_cells = [(0, 1), (0, 2), (1, 1), (1, 0), (2, 0)]
    band = pl.ds(PAD - 1, C + 2)
    for n, (di, dj) in enumerate(corners):
        r0, c0 = (0 if dj < 0 else R - 1), PAD + (0 if di < 0 else C - 1)
        for m, (a, b) in enumerate(near_cells):
            for c in range(3):
                at = c0 + di * b
                SD[n, 3 * m + c : 3 * m + c + 1] = U3[c, q(r0 + dj * a), at : at + 1, :]
    fine = []
    for c in range(3):
        for n in range(3):
            SX[0, c, n] = U3[c, q(-1) : q(R + 1), PAD - n, :]
            SX[1, c, n] = U3[c, q(-1) : q(R + 1), PAD + C - 1 + n, :]
        group = [
            Bundle(None, None, [copy(slot, SX.at[0, c], LX.at[1, c], west, j), copy(slot + 1, SX.at[1, c], LX.at[0, c], east, j)]),
            Bundle(inside(-1), inside(1), [
                copy(slot + 2, U3.at[c, pl.ds(q(-2), 3), band], LR.at[1, c, :, band], i, j - 1),
            ] + (diagonal(slot + 4, SD, LD, -1) if c == 0 else [])),
            Bundle(inside(1), inside(-1), [
                copy(slot + 3, U3.at[c, pl.ds(q(R - 1), 3), band], LR.at[0, c, :, band], i, j + 1),
            ] + (diagonal(slot + 4, SD, LD, 1) if c == 0 else [])),
        ]
        slot = slot + (8 if c == 0 else 4)
        fine.append(group)

    visc_onward.arrive()

    lane_c = lane[:C]

    def repack(get, p):
        s, r = p // rows, p % rows
        a, b = get(s, r % half), get(s + nj // 2, r % half)
        if r >= half:
            a = pltpu.roll(a, LAT - 1, 1)
        else:
            b = pltpu.roll(b, 1, 1)
        return jnp.where(even[: a.shape[0]], a, b)

    def coarse_near(buf, c, p, lo=PAD, width=C):
        part = even[:width]
        block = lambda place, off=0: buf[c, place, lo + off : lo + off + width, :]
        x = block(p)
        below = block(p - 1) if p > 0 else jnp.where(part, 0.0, pltpu.roll(block(packed - 1), 1, 1))
        above = block(p + 1) if p < packed - 1 else jnp.where(part, pltpu.roll(block(0), LAT - 1, 1), 0.0)
        return x, [block(p, -1), block(p, 1), below, above, pltpu.roll(x, 2, 1), pltpu.roll(x, LAT - 2, 1)]

    for p in range(packed):
        CG[0, p] = repack(lambda s, r: LV[s, r], p)
    for p in range(packed):
        v, vn = coarse_near(CG, 0, p)
        vn[4] = jnp.where(lane_c < 2, 0.0, vn[4])
        vn[5] = jnp.where(lane_c >= LAT - 2, 0.0, vn[5])
        coefs = [(v + item) * 0.5 for item in vn]
        diag = coefs[0] + coefs[1] + coefs[2] + coefs[3] + coefs[4] + coefs[5]
        inv = 0.8 / diag
        coefs[4] = jnp.where(lane_c < 2, 0.0, coefs[4])
        coefs[5] = jnp.where(lane_c >= LAT - 2, 0.0, coefs[5])
        for k in range(6):
            CW[k, p] = coefs[k] * inv
        CW[6, p] = 4.0 * inv

    for r in range(half + 1):
        for c in range(3):
            GO[j + 1, c, r] = CP[c, r]

    col = lax.broadcasted_iota(jnp.int32, (C, LAT), 0)
    own = (col >= strip - 1) & (col <= strip + cols)
    before, after = col <= strip, col >= strip + cols - 1

    def total(s, c, p):
        x = jnp.where(own, GO[s + 1, c, p], 0.0)
        return x + jnp.where(before, GW[s + 1, c, p], 0.0) + jnp.where(after, GE[s + 1, c, p], 0.0)

    even_c = even[:C]

    def coarse_part(s, c, r):
        b = total(s, c, r)
        if r == 0 and s > 0:
            b = b + jnp.where(even_c, total(s - 1, c, half), 0.0)
        if r == half - 1 and s < nj - 1:
            b = b + jnp.where(even_c, 0.0, total(s + 1, c, half))
        return b

    def coarse_sweep(src, dst, rim):
        near_rim = 2 * rim <= PAD and cols % 8 == 0
        lo = 2 * strip - PAD // 2 if near_rim else PAD
        width = cols + PAD if near_rim else C
        for p in range(packed):
            for c in range(3):
                x, xn = coarse_near(src, c, p, lo, width)
                t = CB[c, p, lo - PAD : lo - PAD + width, :] + 0.2 * x
                for k in range(6):
                    t = t + CW[k, p, lo - PAD : lo - PAD + width, :] * xn[k]
                dst[c, p, lo : lo + width, :] = t

    def hand_on(c):
        coarse_res[c][0].arrive()
        coarse_res[c][1].start()

    hand_on(0)
    for c in range(3):
        for item in fine[c]:
            item.start()
    hand_on(1)
    hand_on(2)
    for c in range(3):
        coarse_res[c][1].arrive()
    for p in range(packed):
        for c in range(3):
            b = repack(lambda s, r: coarse_part(s, c, r), p) * CW[6, p]
            CB[c, p] = b
            EA[c, p, PAD : PAD + C, :] = b
    src, dst = EA, EB
    for number in range(NC - 1):
        coarse_sweep(src, dst, NC - 1 - number)
        src, dst = dst, src
    wide = EX.shape[2] // 2
    start = 2 * strip - PAD // 2
    for m in range(-1, rows + 1):
        at = rows * j + m
        upper = (at >= packed).astype(jnp.int32)
        valid = parity[:wide] == upper
        for c in range(3):
            x = src[c, lax.rem(at + packed, packed), start : start + wide, :]
            other = jnp.where(upper == 1, pltpu.roll(x, LAT - 1, 1), pltpu.roll(x, 1, 1))
            x = jnp.where(valid, x, other)
            EX[c, m + 1, pl.ds(0, wide, 2), :] = x
            EX[c, m + 1, pl.ds(1, wide, 2), :] = x

    def from_above(c):
        for n in range(3):
            U3[c, q(R - 2 + n), band, :] += LR[1, c, n, band, :]

    def from_below(c):
        for n in range(3):
            U3[c, q(-1 + n), band, :] += LR[0, c, n, band, :]

    def add_corner(c, n, di, dj):
        r0, c0 = (R if dj < 0 else -1), PAD + (C if di < 0 else -1)
        for m, (a, b) in enumerate(near_cells):
            at = c0 + di * b
            U3[c, q(r0 + dj * a), at : at + 1, :] += LD[n, 3 * m + c : 3 * m + c + 1]

    for c in range(3):
        for item in fine[c]:
            item.arrive()
            item.leave()
        for n in range(3):
            U3[c, q(-1) : q(R + 1), PAD + C - n, :] += LX[1, c, n]
            U3[c, q(-1) : q(R + 1), PAD - 1 + n, :] += LX[0, c, n]

        @pl.when(j < nj - 1)
        def _():
            from_above(c)
            for n, (di, dj) in enumerate(corners):
                if dj < 0:
                    add_corner(c, n, di, dj)

        @pl.when(j > 0)
        def _():
            from_below(c)
            for n, (di, dj) in enumerate(corners):
                if dj > 0:
                    add_corner(c, n, di, dj)

    for r in range(-1, R + 1):
        for c in range(3):
            x = EX[c, r // 2 + 1, lo:hi, :]
            xn = [
                EX[c, r // 2 + 1, lo - 1 : hi - 1, :],
                EX[c, r // 2 + 1, lo + 1 : hi + 1, :],
                EX[c, (r - 1) // 2 + 1, lo:hi, :],
                EX[c, (r + 1) // 2 + 1, lo:hi, :],
                pltpu.roll(x, 1, 1),
                pltpu.roll(x, LAT - 1, 1),
            ]
            t = U3[c, q(r), lo:hi, :] + 0.2 * x
            for k in range(6):
                t = t + WT[k, r + 1, lo:hi, :] * xn[k]
            U4[c, q(r), lo:hi, :] = t
    for r in range(R):
        for c in range(3):
            x, t = change(U4, c, r)
            out_ref[c, r] = x + t
    for item in round0:
        item.leave()
    for pair in [(visc_direct, visc_onward)] + coarse_res:
        for item in pair:
            item.leave()


def deliver(tn_ref, out_ref, tn_hbm, out_hbm, sems):
    copies = [pltpu.make_async_copy(tn_ref, tn_hbm, sems.at[0]), pltpu.make_async_copy(out_ref, out_hbm, sems.at[1])]
    for item in copies:
        item.start()
    for item in copies:
        item.wait()


def solution(mesh):
    ni, nj = mesh.shape["lon"], mesh.shape["rad"]

    def local(adjoint_temp, viscosity, velocity, misfit_force, adjoint_guess):
        R, C, LAT = adjoint_temp.shape
        half, cols, wide = R // 4, C // 2, C + 2 * PAD
        f32 = jnp.float32
        frame = lambda n, rows: pltpu.VMEM((n, rows, wide, LAT), f32)
        block = lambda *dims: pltpu.VMEM(dims + (C, LAT), f32)
        copies = 26 + 4 * (3 * nj - 1)
        deep = R + 2 * DEEP
        vmem, place = pl.BlockSpec(memory_space=pltpu.VMEM), pl.BlockSpec(memory_space=pl.ANY)
        P8 = half * nj
        results = pl.pallas_call(
            functools.partial(kernel, ni, nj),
            out_shape=(
                pltpu.VMEM(adjoint_temp.shape, f32),
                pltpu.VMEM(adjoint_guess.shape, f32),
            ),
            in_specs=[place] * 5,
            out_specs=(vmem, vmem),
            scratch_shapes=[
                block(3, R), block(3, R), pltpu.SemaphoreType.DMA((5,)),
                frame(5, deep), frame(3, deep), frame(3, deep), frame(3, deep), frame(3, deep),
                frame(6, R + 2), frame(3, R + 2), pltpu.VMEM((R + 2, wide, LAT), f32), pltpu.VMEM((R + 2, wide, LAT), f32), frame(2, 2),
                pltpu.VMEM((3, 2 * half + 2, C + PAD, LAT), f32), block(2 * half),
                block(3, half + 1), pltpu.VMEM((1, half, cols, LAT), f32),
                block(nj + 2, 3, half + 1), block(nj + 2, 3, half + 1), block(nj + 2, 3, half + 1),
                pltpu.VMEM((nj, half, wide, LAT), f32), frame(1, P8), block(7, P8), block(3, P8),
                frame(3, P8), frame(3, P8), frame(3, 2 * half + 2),
                pltpu.VMEM((2, 7, R, LAT), f32), pltpu.VMEM((2, 7, R, LAT), f32),
                pltpu.VMEM((4, 3, LAT), f32), pltpu.VMEM((4, 3, LAT), f32),
                pltpu.VMEM((2, 3, 3, R + 2, LAT), f32), pltpu.VMEM((2, 3, 3, R + 2, LAT), f32),
                pltpu.VMEM((2, 3, 3, wide, LAT), f32),
                pltpu.VMEM((4, 15, LAT), f32), pltpu.VMEM((4, 15, LAT), f32),
                pltpu.SemaphoreType.DMA((copies,)), pltpu.SemaphoreType.DMA((copies,)),
            ],
            compiler_params=pltpu.CompilerParams(collective_id=0, has_side_effects=True),
        )(adjoint_temp, viscosity, velocity, misfit_force, adjoint_guess)
        return pl.pallas_call(
            deliver,
            out_shape=(jax.ShapeDtypeStruct(adjoint_temp.shape, f32), jax.ShapeDtypeStruct(adjoint_guess.shape, f32)),
            in_specs=[vmem] * 2,
            out_specs=(place, place),
            scratch_shapes=[pltpu.SemaphoreType.DMA((2,))],
        )(*[pltpu.with_memory_space_constraint(item, pltpu.VMEM) for item in results])

    flat = P("rad", "lon", None)
    full = P(None, "rad", "lon", None)
    return jax.shard_map(local, mesh=mesh, in_specs=(flat, flat, full, full, full), out_specs=(flat, full), check_vma=False)
```

```python
import functools

import jax
import jax.numpy as jnp
from jax import lax
from jax.experimental import pallas as pl
from jax.experimental.pallas import tpu as pltpu
from jax.sharding import PartitionSpec as P

NU = 2
NC = 8
PAD = 8
DEEP = 3
MESH = pl.DeviceIdType.MESH


def kernel(ni, nj, temp_hbm, visc_hbm, vel_hbm, mis_hbm, guess_hbm, tn_ref, out_ref,
           vel_ref, mis_ref, local,
           W0, U1, U2, U3, U4, WT, B, D, INV, WF, RS, RV, CP, CV, GO, GW, GE, LV, CG, CW, CB, EA, EB, EX,
           S0, L0, SC, LC, SX, LX, LR, SD, LD, send, recv):
    R, C, LAT = temp_hbm.shape
    half = R // 4
    cols = C // 2
    strip = PAD
    rows = 2 * half
    i = lax.axis_index("lon")
    j = lax.axis_index("rad")
    west, east = lax.rem(i + ni - 1, ni), lax.rem(i + 1, ni)

    q = lambda r: r + DEEP
    mid = pl.ds(PAD, C)
    inner = pl.ds(DEEP, R)
    loads = [
        pltpu.make_async_copy(visc_hbm, W0.at[4, inner, mid], local.at[0]),
        pltpu.make_async_copy(temp_hbm, W0.at[3, inner, mid], local.at[1]),
        pltpu.make_async_copy(guess_hbm, W0.at[0:3, inner, mid], local.at[2]),
        pltpu.make_async_copy(vel_hbm, vel_ref, local.at[3]),
        pltpu.make_async_copy(mis_hbm, mis_ref, local.at[4]),
    ]
    for item in loads:
        item.start()

    barrier = pltpu.get_barrier_semaphore()
    for d in range(nj):
        other = lax.rem(j + d, nj)
        for lon in (west, east) if d == 0 else (west, east, i):
            pl.semaphore_signal(barrier, inc=1, device_id={"lon": lon, "rad": other}, device_id_type=MESH)

    lo, hi = PAD // 2, C + PAD + PAD // 2
    span = hi - lo
    lane_all = lax.broadcasted_iota(jnp.int32, (C + 2 * PAD, LAT), 1)
    lane = lane_all[:span]
    first, last = lane == 0, lane == LAT - 1
    parity = lax.rem(lane_all, 2)
    even = parity == 0

    edges = (pl.ds(0, PAD), pl.ds(PAD + C, PAD))
    for edge in edges:
        W0[4, :, edge, :] = jnp.ones_like(W0[4, :, edge, :])
        for buf in (B, U1, U2):
            buf[:, :, edge, :] = jnp.zeros_like(buf[:, :, edge, :])
    for c in range(3):
        for r in (0, R + 1):
            B[c, r, mid, :] = jnp.zeros((C, LAT), jnp.float32)
        for r in (-2, -1, R, R + 1):
            U1[c, q(r), mid, :] = jnp.zeros((C, LAT), jnp.float32)
        for r in (-2, R + 1):
            U2[c, q(r), mid, :] = jnp.zeros((C, LAT), jnp.float32)
    packed = half * nj
    for buf in (EA, EB):
        buf[...] = jnp.zeros_like(buf)

    def halves(a, b):
        a = a + pltpu.roll(a, LAT - 1, 1)
        b = b + pltpu.roll(b, 1, 1)
        return 0.125 * jnp.where(even[: a.shape[0]], a, b)

    def under(cond, action):
        if cond is None:
            action()
        else:
            pl.when(cond)(action)

    def copy(slot, src, dst, lon, rad):
        return pltpu.make_async_remote_copy(
            src_ref=src, dst_ref=dst, send_sem=send.at[slot], recv_sem=recv.at[slot],
            device_id={"lon": lon, "rad": rad}, device_id_type=MESH)

    class Bundle:
        def __init__(self, to, came, items):
            self.to, self.came, self.items = to, came, items

        def each(self, cond, act):
            def action():
                for item in self.items:
                    act(item)
            under(cond, action)

        def start(self):
            self.each(self.to, lambda item: item.start())

        def arrive(self):
            self.each(self.came, lambda item: item.wait_recv())

        def leave(self):
            self.each(self.to, lambda item: item.wait_send())

    inside = lambda d: (None if d == 0 else (j + d >= 0) & (j + d < nj))
    corners = [(di, dj) for di in (-1, 1) for dj in (-1, 1)]
    at_lon = {-1: west, 0: i, 1: east}

    loads[0].wait()
    for p in range(rows):
        RV[p] = W0[4, q(2 * p), mid, :] + W0[4, q(2 * p + 1), mid, :]
    for r in range(half):
        a = RV[r, pl.ds(0, cols, 2), :] + RV[r, pl.ds(1, cols, 2), :]
        b = RV[r + half, pl.ds(0, cols, 2), :] + RV[r + half, pl.ds(1, cols, 2), :]
        CV[0, r] = halves(a, b)
    for n in range(3):
        S0[0, 4 + n] = W0[4, inner, PAD + n, :]
        S0[1, 4 + n] = W0[4, inner, PAD + C - 1 - n, :]
    for n, (di, dj) in enumerate(corners):
        r0, c0 = (0 if dj < 0 else R - 1), PAD + (0 if di < 0 else C - 1)
        SC[n, 0:1] = W0[4, q(r0), c0 : c0 + 1, :]
        SC[n, 1:2] = W0[4, q(r0), c0 - di : c0 - di + 1, :]
        SC[n, 2:3] = W0[4, q(r0 - dj), c0 : c0 + 1, :]
    loads[1].wait()
    loads[2].wait()
    for c in range(4):
        S0[0, c] = W0[c, inner, PAD, :]
        S0[1, c] = W0[c, inner, PAD + C - 1, :]
    pl.semaphore_wait(barrier, 3 * nj - 1)

    round0 = [Bundle(None, None, [copy(0, S0.at[0], L0.at[1], west, j), copy(1, S0.at[1], L0.at[0], east, j)])]
    diagonal = lambda slot, src, dst, dj: [
        copy(slot + n, src.at[n], dst.at[n], at_lon[di], j + dj) for n, (di, d) in enumerate(corners) if d == dj]
    round0.append(Bundle(inside(-1), inside(1), [
        copy(2, W0.at[:, q(0), mid], W0.at[:, q(R), mid], i, j - 1),
        copy(3, W0.at[4, pl.ds(q(1), 2), mid], W0.at[4, pl.ds(q(R + 1), 2), mid], i, j - 1),
    ] + diagonal(6, SC, LC, -1)))
    round0.append(Bundle(inside(1), inside(-1), [
        copy(4, W0.at[:, q(R - 1), mid], W0.at[:, q(-1), mid], i, j + 1),
        copy(5, W0.at[4, pl.ds(q(R - 3), 2), mid], W0.at[4, pl.ds(q(-3), 2), mid], i, j + 1),
    ] + diagonal(6, SC, LC, 1)))
    for item in round0:
        item.start()

    other_core = j + 1 - 2 * lax.rem(j, 2)
    alike = [lax.rem(j + 2 * k, nj) for k in range(1, nj // 2)]
    legs = 3 * nj - 1

    def relay(slot, src, dst):
        route = [(di, j, src[di], dst[di](j)) for di in (-1, 1)]
        route += [(di, rad, src[di], dst[di](j)) for rad in alike for di in (-1, 1, 0)]
        route += [(0, other_core, src[0], dst[0](j))]
        direct = Bundle(None, None, [copy(slot + n, a, b, at_lon[di], rad) for n, (di, rad, a, b) in enumerate(route)])
        slot = slot + len(route)
        hand = [dst[di](j) for di in (-1, 1)] + [dst[di](rad) for rad in alike for di in (-1, 1, 0)]
        onward = Bundle(None, None, [copy(slot + n, ref, ref, i, other_core) for n, ref in enumerate(hand)])
        direct.start()
        return direct, onward

    def visc_place(start, width):
        return lambda rad: LV.at[rad, :, pl.ds(start, width)]

    deep = NC + 1
    visc_direct, visc_onward = relay(10, {
        -1: CV.at[0, :, pl.ds(0, deep)], 0: CV.at[0], 1: CV.at[0, :, pl.ds(cols - deep, deep)],
    }, {
        -1: visc_place(2 * strip + cols, deep), 0: visc_place(2 * strip, cols), 1: visc_place(2 * strip - deep, deep),
    })
    for r in range(half):
        LV[j, r, 2 * strip : 2 * strip + cols, :] = CV[0, r]
    loads[3].wait()
    loads[4].wait()

    def near(buf, c, r, lo=PAD, width=C):
        hi = lo + width
        x = buf[c, q(r), lo:hi, :]
        return x, [
            buf[c, q(r), lo - 1 : hi - 1, :],
            buf[c, q(r), lo + 1 : hi + 1, :],
            buf[c, q(r - 1), lo:hi, :],
            buf[c, q(r + 1), lo:hi, :],
            pltpu.roll(x, 1, 1),
            pltpu.roll(x, LAT - 1, 1),
        ]

    def faces(r, a=lo, n=span):
        v, vn = near(W0, 4, r, a, n)
        vn[4] = jnp.where(first[:n], 0.0, vn[4])
        vn[5] = jnp.where(last[:n], 0.0, vn[5])
        coefs = [(v + item) * 0.5 for item in vn]
        diag = coefs[0] + coefs[1] + coefs[2] + coefs[3] + coefs[4] + coefs[5]
        return coefs, diag, 0.8 / diag

    def set_weights(r, a=lo, n=span):
        coefs, diag, inv = faces(r, a, n)
        coefs[4] = jnp.where(first[:n], 0.0, coefs[4])
        coefs[5] = jnp.where(last[:n], 0.0, coefs[5])
        for k in range(6):
            WT[k, r + 1, a : a + n, :] = coefs[k] * inv
        D[r + 1, a : a + n, :] = diag * 1.25
        INV[r + 1, a : a + n, :] = inv

    def set_rhs(r, a=PAD, n=C):
        inv = INV[r + 1, a : a + n, :]
        at = slice(a - PAD, a - PAD + n)
        t, tn = near(W0, 3, r, a, n)
        tn[4] = jnp.where(first[:n], 0.0, tn[4])
        tn[5] = jnp.where(last[:n], 0.0, tn[5])
        advect = vel_ref[0, r, at] * (tn[3] - tn[2]) + vel_ref[1, r, at] * (tn[1] - tn[0]) + vel_ref[2, r, at] * (tn[5] - tn[4])
        spread_t = tn[0] + tn[1] + tn[2] + tn[3] + tn[4] + tn[5] - 6.0 * t
        t_next = t + 0.125 * advect + 0.1 * spread_t
        tn_ref[r, at] = t_next
        B[0, r + 1, a : a + n, :] = (mis_ref[0, r, at] + t_next) * inv
        B[1, r + 1, a : a + n, :] = mis_ref[1, r, at] * inv
        B[2, r + 1, a : a + n, :] = mis_ref[2, r, at] * inv

    def change(buf, c, r, lo=PAD, width=C):
        x, xn = near(buf, c, r, lo, width)
        t = B[c, r + 1, lo : lo + width, :] - 0.8 * x
        for k in range(6):
            t = t + WT[k, r + 1, lo : lo + width, :] * xn[k]
        return x, t

    def sweep_to(dst, src, c, r, a, n):
        x, t = change(src, c, r, a, n)
        dst[c, q(r), a : a + n, :] = x + t

    outer = [(lo, PAD), (hi - PAD, PAD)]
    outer_own = [(PAD, PAD // 2), (hi - PAD, PAD // 2)]
    calm = range(1, R - 1)
    calmer = range(2, R - 2)
    rest = lambda some, which: [r for r in some if r not in which]
    for r in calm:
        set_weights(r)
        set_rhs(r)
    for r in calm:
        for c in range(3):
            sweep_to(U1, W0, c, r, PAD, C)
    for r in calmer:
        for c in range(3):
            sweep_to(U2, U1, c, r, lo, span)

    for item in round0:
        item.arrive()
    for c in range(4):
        W0[c, inner, PAD - 1, :] = L0[0, c]
        W0[c, inner, PAD + C, :] = L0[1, c]
    for n in range(3):
        W0[4, inner, PAD - 1 - n, :] = L0[0, 4 + n]
        W0[4, inner, PAD + C + n, :] = L0[1, 4 + n]
    for n, (di, dj) in enumerate(corners):
        rr, cc = (R if dj < 0 else -1), PAD + (C if di < 0 else -1)
        def place_corner(n=n, di=di, dj=dj, rr=rr, cc=cc):
            W0[4, q(rr), cc : cc + 1, :] = LC[n, 0:1]
            W0[4, q(rr), cc - di : cc - di + 1, :] = LC[n, 1:2]
            W0[4, q(rr - dj), cc : cc + 1, :] = LC[n, 2:3]
        pl.when(inside(-dj))(place_corner)

    @pl.when(j == 0)
    def _():
        W0[:, q(-1)] = jnp.zeros_like(W0[:, q(-1)])
        W0[4, q(-3) : q(-1)] = jnp.ones_like(W0[4, q(-3) : q(-1)])

    @pl.when(j == nj - 1)
    def _():
        W0[:, q(R)] = jnp.zeros_like(W0[:, q(R)])
        W0[4, q(R + 1) : q(R + 3)] = jnp.ones_like(W0[4, q(R + 1) : q(R + 3)])

    for r in rest(range(-1, R + 1), calm):
        set_weights(r)
    for r in calm:
        for a, n in outer:
            set_weights(r, a, n)
    for n, (r, k) in enumerate(((-2, 3), (R + 1, 2))):
        coefs, diag, inv = faces(r)
        WF[0, n, lo:hi, :] = coefs[k] * inv
        WF[1, n, lo:hi, :] = coefs[k]
    for r in rest(range(R), calm):
        set_rhs(r)
    for r in calm:
        for a, n in outer_own:
            set_rhs(r, a, n)

    @pl.when(j == 0)
    def _():
        WT[2, 1] = jnp.zeros_like(WT[2, 1])
        WT[:, 0] = jnp.zeros_like(WT[:, 0])

    @pl.when(j == nj - 1)
    def _():
        WT[3, R] = jnp.zeros_like(WT[3, R])
        WT[:, R + 1] = jnp.zeros_like(WT[:, R + 1])

    for c in range(3):
        for r in rest(range(R), calm):
            sweep_to(U1, W0, c, r, PAD, C)
        for r in calm:
            for a, n in outer_own:
                sweep_to(U1, W0, c, r, a, n)

    def residual(c, r):
        x, t = change(U2, c, r, lo, span)
        U3[c, q(r), lo:hi, :] = x + t
        return D[r + 1, lo:hi, :] * t

    def part(c, slot):
        width = NC + 1
        place = lambda buf, start, size: lambda rad: buf.at[rad + 1, c, :, pl.ds(start, size)]
        return relay(slot, {
            -1: CP.at[c, :, pl.ds(strip - 1, width)],
            0: CP.at[c, :, pl.ds(strip - 1, cols + 2)],
            1: CP.at[c, :, pl.ds(strip + cols - NC, width)],
        }, {
            -1: place(GE, strip - 1 + cols, width),
            0: place(GO, strip - 1, cols + 2),
            1: place(GW, strip - NC, width),
        })

    wide_c = span // 2
    slot = 10 + legs
    coarse_res = []
    for c in range(3):
        U2[c, q(-1), mid, :] = WT[3, 0, mid, :] * U1[c, q(0), mid, :]
        U2[c, q(R), mid, :] = WT[2, R + 1, mid, :] * U1[c, q(R - 1), mid, :]
        for r in rest(range(R), calmer):
            sweep_to(U2, U1, c, r, lo, span)
        for r in calmer:
            for a, n in outer:
                sweep_to(U2, U1, c, r, a, n)
        for r, k, p in ((-2, 3, 0), (R + 1, 2, rows + 1)):
            other = -1 if r < 0 else R
            x = U2[c, q(other), lo:hi, :]
            U3[c, q(r), lo:hi, :] = WF[0, int(p > 0), lo:hi, :] * x
            RS[c, p] = WF[1, int(p > 0), lo:hi, :] * x + residual(c, other)
        for p in range(rows):
            RS[c, p + 1] = residual(c, 2 * p) + residual(c, 2 * p + 1)
        pair = lambda p: RS[c, p + 1, pl.ds(0, wide_c, 2), :] + RS[c, p + 1, pl.ds(1, wide_c, 2), :]
        for r, a, b in [(r, r, r + half) for r in range(half)] + [(half, rows, -1)]:
            CP[c, r, strip - 2 : strip - 2 + wide_c, :] = halves(pair(a), pair(b))
        coarse_res.append(part(c, slot))
        slot = slot + legs
        if c == 0:
            visc_direct.arrive()
            visc_onward.start()

    near_cells = [(0, 1), (0, 2), (1, 1), (1, 0), (2, 0)]
    band = pl.ds(PAD - 1, C + 2)
    for n, (di, dj) in enumerate(corners):
        r0, c0 = (0 if dj < 0 else R - 1), PAD + (0 if di < 0 else C - 1)
        for m, (a, b) in enumerate(near_cells):
            for c in range(3):
                at = c0 + di * b
                SD[n, 3 * m + c : 3 * m + c + 1] = U3[c, q(r0 + dj * a), at : at + 1, :]
    fine = []
    for c in range(3):
        for n in range(3):
            SX[0, c, n] = U3[c, q(-1) : q(R + 1), PAD - n, :]
            SX[1, c, n] = U3[c, q(-1) : q(R + 1), PAD + C - 1 + n, :]
        group = [
            Bundle(None, None, [copy(slot, SX.at[0, c], LX.at[1, c], west, j), copy(slot + 1, SX.at[1, c], LX.at[0, c], east, j)]),
            Bundle(inside(-1), inside(1), [
                copy(slot + 2, U3.at[c, pl.ds(q(-2), 3), band], LR.at[1, c, :, band], i, j - 1),
            ] + (diagonal(slot + 4, SD, LD, -1) if c == 0 else [])),
            Bundle(inside(1), inside(-1), [
                copy(slot + 3, U3.at[c, pl.ds(q(R - 1), 3), band], LR.at[0, c, :, band], i, j + 1),
            ] + (diagonal(slot + 4, SD, LD, 1) if c == 0 else [])),
        ]
        slot = slot + (8 if c == 0 else 4)
        fine.append(group)

    visc_onward.arrive()

    lane_c = lane[:C]

    def repack(get, p):
        s, r = p // rows, p % rows
        a, b = get(s, r % half), get(s + nj // 2, r % half)
        if r >= half:
            a = pltpu.roll(a, LAT - 1, 1)
        else:
            b = pltpu.roll(b, 1, 1)
        return jnp.where(even[: a.shape[0]], a, b)

    def coarse_near(buf, c, p, lo=PAD, width=C):
        part = even[:width]
        block = lambda place, off=0: buf[c, place, lo + off : lo + off + width, :]
        x = block(p)
        below = block(p - 1) if p > 0 else jnp.where(part, 0.0, pltpu.roll(block(packed - 1), 1, 1))
        above = block(p + 1) if p < packed - 1 else jnp.where(part, pltpu.roll(block(0), LAT - 1, 1), 0.0)
        return x, [block(p, -1), block(p, 1), below, above, pltpu.roll(x, 2, 1), pltpu.roll(x, LAT - 2, 1)]

    for p in range(packed):
        CG[0, p] = repack(lambda s, r: LV[s, r], p)
    for p in range(packed):
        v, vn = coarse_near(CG, 0, p)
        vn[4] = jnp.where(lane_c < 2, 0.0, vn[4])
        vn[5] = jnp.where(lane_c >= LAT - 2, 0.0, vn[5])
        coefs = [(v + item) * 0.5 for item in vn]
        diag = coefs[0] + coefs[1] + coefs[2] + coefs[3] + coefs[4] + coefs[5]
        inv = 0.8 / diag
        coefs[4] = jnp.where(lane_c < 2, 0.0, coefs[4])
        coefs[5] = jnp.where(lane_c >= LAT - 2, 0.0, coefs[5])
        for k in range(6):
            CW[k, p] = coefs[k] * inv
        CW[6, p] = 4.0 * inv

    for r in range(half + 1):
        for c in range(3):
            GO[j + 1, c, r] = CP[c, r]

    col = lax.broadcasted_iota(jnp.int32, (C, LAT), 0)
    own = (col >= strip - 1) & (col <= strip + cols)
    before, after = col <= strip, col >= strip + cols - 1

    def total(s, c, p):
        x = jnp.where(own, GO[s + 1, c, p], 0.0)
        return x + jnp.where(before, GW[s + 1, c, p], 0.0) + jnp.where(after, GE[s + 1, c, p], 0.0)

    even_c = even[:C]

    def coarse_part(s, c, r):
        b = total(s, c, r)
        if r == 0 and s > 0:
            b = b + jnp.where(even_c, total(s - 1, c, half), 0.0)
        if r == half - 1 and s < nj - 1:
            b = b + jnp.where(even_c, 0.0, total(s + 1, c, half))
        return b

    def coarse_sweep(src, dst, rim):
        near_rim = 2 * rim <= PAD and cols % 8 == 0
        lo = 2 * strip - PAD // 2 if near_rim else PAD
        width = cols + PAD if near_rim else C
        for p in range(packed):
            for c in range(3):
                x, xn = coarse_near(src, c, p, lo, width)
                t = CB[c, p, lo - PAD : lo - PAD + width, :] + 0.2 * x
                for k in range(6):
                    t = t + CW[k, p, lo - PAD : lo - PAD + width, :] * xn[k]
                dst[c, p, lo : lo + width, :] = t

    def hand_on(c):
        coarse_res[c][0].arrive()
        coarse_res[c][1].start()

    hand_on(0)
    for c in range(3):
        for item in fine[c]:
            item.start()
    hand_on(1)
    hand_on(2)
    for c in range(3):
        coarse_res[c][1].arrive()
    for p in range(packed):
        for c in range(3):
            b = repack(lambda s, r: coarse_part(s, c, r), p) * CW[6, p]
            CB[c, p] = b
            EA[c, p, PAD : PAD + C, :] = b
    src, dst = EA, EB
    for number in range(NC - 1):
        coarse_sweep(src, dst, NC - 1 - number)
        src, dst = dst, src
    wide = EX.shape[2] // 2
    start = 2 * strip - PAD // 2
    for m in range(-1, rows + 1):
        at = rows * j + m
        upper = (at >= packed).astype(jnp.int32)
        valid = parity[:wide] == upper
        for c in range(3):
            x = src[c, lax.rem(at + packed, packed), start : start + wide, :]
            other = jnp.where(upper == 1, pltpu.roll(x, LAT - 1, 1), pltpu.roll(x, 1, 1))
            x = jnp.where(valid, x, other)
            EX[c, m + 1, pl.ds(0, wide, 2), :] = x
            EX[c, m + 1, pl.ds(1, wide, 2), :] = x

    def from_above(c):
        for n in range(3):
            U3[c, q(R - 2 + n), band, :] += LR[1, c, n, band, :]

    def from_below(c):
        for n in range(3):
            U3[c, q(-1 + n), band, :] += LR[0, c, n, band, :]

    def add_corner(c, n, di, dj):
        r0, c0 = (R if dj < 0 else -1), PAD + (C if di < 0 else -1)
        for m, (a, b) in enumerate(near_cells):
            at = c0 + di * b
            U3[c, q(r0 + dj * a), at : at + 1, :] += LD[n, 3 * m + c : 3 * m + c + 1]

    for c in range(3):
        for item in fine[c]:
            item.arrive()
            item.leave()
        for n in range(3):
            U3[c, q(-1) : q(R + 1), PAD + C - n, :] += LX[1, c, n]
            U3[c, q(-1) : q(R + 1), PAD - 1 + n, :] += LX[0, c, n]

        @pl.when(j < nj - 1)
        def _():
            from_above(c)
            for n, (di, dj) in enumerate(corners):
                if dj < 0:
                    add_corner(c, n, di, dj)

        @pl.when(j > 0)
        def _():
            from_below(c)
            for n, (di, dj) in enumerate(corners):
                if dj > 0:
                    add_corner(c, n, di, dj)

    for r in range(-1, R + 1):
        for c in range(3):
            x = EX[c, r // 2 + 1, lo:hi, :]
            xn = [
                EX[c, r // 2 + 1, lo - 1 : hi - 1, :],
                EX[c, r // 2 + 1, lo + 1 : hi + 1, :],
                EX[c, (r - 1) // 2 + 1, lo:hi, :],
                EX[c, (r + 1) // 2 + 1, lo:hi, :],
                pltpu.roll(x, 1, 1),
                pltpu.roll(x, LAT - 1, 1),
            ]
            t = U3[c, q(r), lo:hi, :] + 0.2 * x
            for k in range(6):
                t = t + WT[k, r + 1, lo:hi, :] * xn[k]
            U4[c, q(r), lo:hi, :] = t
    for r in range(R):
        for c in range(3):
            x, t = change(U4, c, r)
            out_ref[c, r] = x + t
    for item in round0:
        item.leave()
    for pair in [(visc_direct, visc_onward)] + coarse_res:
        for item in pair:
            item.leave()


def deliver(tn_ref, out_ref, tn_hbm, out_hbm, sems):
    copies = [pltpu.make_async_copy(tn_ref, tn_hbm, sems.at[0]), pltpu.make_async_copy(out_ref, out_hbm, sems.at[1])]
    for item in copies:
        item.start()
    for item in copies:
        item.wait()


def solution(mesh):
    ni, nj = mesh.shape["lon"], mesh.shape["rad"]

    def local(adjoint_temp, viscosity, velocity, misfit_force, adjoint_guess):
        R, C, LAT = adjoint_temp.shape
        half, cols, wide = R // 4, C // 2, C + 2 * PAD
        f32 = jnp.float32
        frame = lambda n, rows: pltpu.VMEM((n, rows, wide, LAT), f32)
        block = lambda *dims: pltpu.VMEM(dims + (C, LAT), f32)
        copies = 26 + 4 * (3 * nj - 1)
        deep = R + 2 * DEEP
        vmem, place = pl.BlockSpec(memory_space=pltpu.VMEM), pl.BlockSpec(memory_space=pl.ANY)
        P8 = half * nj
        results = pl.pallas_call(
            functools.partial(kernel, ni, nj),
            out_shape=(
                pltpu.VMEM(adjoint_temp.shape, f32),
                pltpu.VMEM(adjoint_guess.shape, f32),
            ),
            in_specs=[place] * 5,
            out_specs=(vmem, vmem),
            scratch_shapes=[
                block(3, R), block(3, R), pltpu.SemaphoreType.DMA((5,)),
                frame(5, deep), frame(3, deep), frame(3, deep), frame(3, deep), frame(3, deep),
                frame(6, R + 2), frame(3, R + 2), pltpu.VMEM((R + 2, wide, LAT), f32), pltpu.VMEM((R + 2, wide, LAT), f32), frame(2, 2),
                pltpu.VMEM((3, 2 * half + 2, C + PAD, LAT), f32), block(2 * half),
                block(3, half + 1), pltpu.VMEM((1, half, cols, LAT), f32),
                block(nj + 2, 3, half + 1), block(nj + 2, 3, half + 1), block(nj + 2, 3, half + 1),
                pltpu.VMEM((nj, half, wide, LAT), f32), frame(1, P8), block(7, P8), block(3, P8),
                frame(3, P8), frame(3, P8), frame(3, 2 * half + 2),
                pltpu.VMEM((2, 7, R, LAT), f32), pltpu.VMEM((2, 7, R, LAT), f32),
                pltpu.VMEM((4, 3, LAT), f32), pltpu.VMEM((4, 3, LAT), f32),
                pltpu.VMEM((2, 3, 3, R + 2, LAT), f32), pltpu.VMEM((2, 3, 3, R + 2, LAT), f32),
                pltpu.VMEM((2, 3, 3, wide, LAT), f32),
                pltpu.VMEM((4, 15, LAT), f32), pltpu.VMEM((4, 15, LAT), f32),
                pltpu.SemaphoreType.DMA((copies,)), pltpu.SemaphoreType.DMA((copies,)),
            ],
            compiler_params=pltpu.CompilerParams(collective_id=0, has_side_effects=True),
        )(adjoint_temp, viscosity, velocity, misfit_force, adjoint_guess)
        return pl.pallas_call(
            deliver,
            out_shape=(jax.ShapeDtypeStruct(adjoint_temp.shape, f32), jax.ShapeDtypeStruct(adjoint_guess.shape, f32)),
            in_specs=[vmem] * 2,
            out_specs=(place, place),
            scratch_shapes=[pltpu.SemaphoreType.DMA((2,))],
        )(*[pltpu.with_memory_space_constraint(item, pltpu.VMEM) for item in results])

    flat = P("rad", "lon", None)
    full = P(None, "rad", "lon", None)
    return jax.shard_map(local, mesh=mesh, in_specs=(flat, flat, full, full, full), out_specs=(flat, full), check_vma=False)
```

```python
import functools

import jax
import jax.numpy as jnp
from jax import lax
from jax.experimental import pallas as pl
from jax.experimental.pallas import tpu as pltpu
from jax.sharding import PartitionSpec as P

NU = 2
NC = 8
PAD = 8
DEEP = 3
MESH = pl.DeviceIdType.MESH


def kernel(ni, nj, temp_hbm, visc_hbm, vel_hbm, mis_hbm, guess_hbm, tn_ref, out_ref,
           vel_ref, mis_ref, local,
           W0, U1, U2, U3, U4, WT, B, D, INV, WF, RS, RV, CP, CV, GO, GW, GE, LV, CG, CW, CB, EA, EB, EX,
           S0, L0, SC, LC, SX, LX, LR, SD, LD, send, recv):
    R, C, LAT = temp_hbm.shape
    half = R // 4
    cols = C // 2
    strip = PAD
    rows = 2 * half
    i = lax.axis_index("lon")
    j = lax.axis_index("rad")
    west, east = lax.rem(i + ni - 1, ni), lax.rem(i + 1, ni)

    q = lambda r: r + DEEP
    mid = pl.ds(PAD, C)
    inner = pl.ds(DEEP, R)
    loads = [
        pltpu.make_async_copy(visc_hbm, W0.at[4, inner, mid], local.at[0]),
        pltpu.make_async_copy(temp_hbm, W0.at[3, inner, mid], local.at[1]),
        pltpu.make_async_copy(guess_hbm, W0.at[0:3, inner, mid], local.at[2]),
        pltpu.make_async_copy(vel_hbm, vel_ref, local.at[3]),
        pltpu.make_async_copy(mis_hbm, mis_ref, local.at[4]),
    ]
    for item in loads:
        item.start()

    barrier = pltpu.get_barrier_semaphore()
    for d in range(nj):
        other = lax.rem(j + d, nj)
        for lon in (west, east) if d == 0 else (west, east, i):
            pl.semaphore_signal(barrier, inc=1, device_id={"lon": lon, "rad": other}, device_id_type=MESH)

    lo, hi = PAD // 2, C + PAD + PAD // 2
    span = hi - lo
    lane_all = lax.broadcasted_iota(jnp.int32, (C + 2 * PAD, LAT), 1)
    lane = lane_all[:span]
    first, last = lane == 0, lane == LAT - 1
    parity = lax.rem(lane_all, 2)
    even = parity == 0

    edges = (pl.ds(0, PAD), pl.ds(PAD + C, PAD))
    for edge in edges:
        W0[4, :, edge, :] = jnp.ones_like(W0[4, :, edge, :])
        for buf in (B, U1, U2):
            buf[:, :, edge, :] = jnp.zeros_like(buf[:, :, edge, :])
    for c in range(3):
        for r in (0, R + 1):
            B[c, r, mid, :] = jnp.zeros((C, LAT), jnp.float32)
        for r in (-2, -1, R, R + 1):
            U1[c, q(r), mid, :] = jnp.zeros((C, LAT), jnp.float32)
        for r in (-2, R + 1):
            U2[c, q(r), mid, :] = jnp.zeros((C, LAT), jnp.float32)
    packed = half * nj
    for buf in (EA, EB):
        buf[...] = jnp.zeros_like(buf)

    def halves(a, b):
        a = a + pltpu.roll(a, LAT - 1, 1)
        b = b + pltpu.roll(b, 1, 1)
        return 0.125 * jnp.where(even[: a.shape[0]], a, b)

    def under(cond, action):
        if cond is None:
            action()
        else:
            pl.when(cond)(action)

    def copy(slot, src, dst, lon, rad):
        return pltpu.make_async_remote_copy(
            src_ref=src, dst_ref=dst, send_sem=send.at[slot], recv_sem=recv.at[slot],
            device_id={"lon": lon, "rad": rad}, device_id_type=MESH)

    class Bundle:
        def __init__(self, to, came, items):
            self.to, self.came, self.items = to, came, items

        def each(self, cond, act):
            def action():
                for item in self.items:
                    act(item)
            under(cond, action)

        def start(self):
            self.each(self.to, lambda item: item.start())

        def arrive(self):
            self.each(self.came, lambda item: item.wait_recv())

        def leave(self):
            self.each(self.to, lambda item: item.wait_send())

    inside = lambda d: (None if d == 0 else (j + d >= 0) & (j + d < nj))
    corners = [(di, dj) for di in (-1, 1) for dj in (-1, 1)]
    at_lon = {-1: west, 0: i, 1: east}

    loads[0].wait()
    for p in range(rows):
        RV[p] = W0[4, q(2 * p), mid, :] + W0[4, q(2 * p + 1), mid, :]
    for r in range(half):
        a = RV[r, pl.ds(0, cols, 2), :] + RV[r, pl.ds(1, cols, 2), :]
        b = RV[r + half, pl.ds(0, cols, 2), :] + RV[r + half, pl.ds(1, cols, 2), :]
        CV[0, r] = halves(a, b)
    for n in range(3):
        S0[0, 4 + n] = W0[4, inner, PAD + n, :]
        S0[1, 4 + n] = W0[4, inner, PAD + C - 1 - n, :]
    for n, (di, dj) in enumerate(corners):
        r0, c0 = (0 if dj < 0 else R - 1), PAD + (0 if di < 0 else C - 1)
        SC[n, 0:1] = W0[4, q(r0), c0 : c0 + 1, :]
        SC[n, 1:2] = W0[4, q(r0), c0 - di : c0 - di + 1, :]
        SC[n, 2:3] = W0[4, q(r0 - dj), c0 : c0 + 1, :]
    loads[1].wait()
    loads[2].wait()
    for c in range(4):
        S0[0, c] = W0[c, inner, PAD, :]
        S0[1, c] = W0[c, inner, PAD + C - 1, :]
    pl.semaphore_wait(barrier, 3 * nj - 1)

    round0 = [Bundle(None, None, [copy(0, S0.at[0], L0.at[1], west, j), copy(1, S0.at[1], L0.at[0], east, j)])]
    diagonal = lambda slot, src, dst, count, dj: [
        copy(slot + n, src.at[n, pl.ds(0, count)], dst.at[n, pl.ds(0, count)], at_lon[di], j + dj) for n, (di, d) in enumerate(corners) if d == dj]
    round0.append(Bundle(inside(-1), inside(1), [
        copy(2, W0.at[:, q(0), mid], W0.at[:, q(R), mid], i, j - 1),
        copy(3, W0.at[4, pl.ds(q(1), 2), mid], W0.at[4, pl.ds(q(R + 1), 2), mid], i, j - 1),
    ] + diagonal(6, SC, LC, 3, -1)))
    round0.append(Bundle(inside(1), inside(-1), [
        copy(4, W0.at[:, q(R - 1), mid], W0.at[:, q(-1), mid], i, j + 1),
        copy(5, W0.at[4, pl.ds(q(R - 3), 2), mid], W0.at[4, pl.ds(q(-3), 2), mid], i, j + 1),
    ] + diagonal(6, SC, LC, 3, 1)))
    for item in round0:
        item.start()

    other_core = j + 1 - 2 * lax.rem(j, 2)
    alike = [lax.rem(j + 2 * k, nj) for k in range(1, nj // 2)]
    legs = 3 * nj - 1

    def relay(slot, src, dst):
        route = [(di, j, src[di], dst[di](j)) for di in (-1, 1)]
        route += [(di, rad, src[di], dst[di](j)) for rad in alike for di in (-1, 1, 0)]
        route += [(0, other_core, src[0], dst[0](j))]
        direct = Bundle(None, None, [copy(slot + n, a, b, at_lon[di], rad) for n, (di, rad, a, b) in enumerate(route)])
        slot = slot + len(route)
        hand = [dst[di](j) for di in (-1, 1)] + [dst[di](rad) for rad in alike for di in (-1, 1, 0)]
        onward = Bundle(None, None, [copy(slot + n, ref, ref, i, other_core) for n, ref in enumerate(hand)])
        direct.start()
        return direct, onward

    def visc_place(start, width):
        return lambda rad: LV.at[rad, :, pl.ds(start, width)]

    deep = NC + 1
    visc_direct, visc_onward = relay(10, {
        -1: CV.at[0, :, pl.ds(0, deep)], 0: CV.at[0], 1: CV.at[0, :, pl.ds(cols - deep, deep)],
    }, {
        -1: visc_place(2 * strip + cols, deep), 0: visc_place(2 * strip, cols), 1: visc_place(2 * strip - deep, deep),
    })
    for r in range(half):
        LV[j, r, 2 * strip : 2 * strip + cols, :] = CV[0, r]
    loads[3].wait()
    loads[4].wait()

    def near(buf, c, r, lo=PAD, width=C):
        hi = lo + width
        x = buf[c, q(r), lo:hi, :]
        return x, [
            buf[c, q(r), lo - 1 : hi - 1, :],
            buf[c, q(r), lo + 1 : hi + 1, :],
            buf[c, q(r - 1), lo:hi, :],
            buf[c, q(r + 1), lo:hi, :],
            pltpu.roll(x, 1, 1),
            pltpu.roll(x, LAT - 1, 1),
        ]

    def faces(r, a=lo, n=span):
        v, vn = near(W0, 4, r, a, n)
        vn[4] = jnp.where(first[:n], 0.0, vn[4])
        vn[5] = jnp.where(last[:n], 0.0, vn[5])
        coefs = [(v + item) * 0.5 for item in vn]
        diag = coefs[0] + coefs[1] + coefs[2] + coefs[3] + coefs[4] + coefs[5]
        return coefs, diag, 0.8 / diag

    def set_weights(r, a=lo, n=span):
        coefs, diag, inv = faces(r, a, n)
        coefs[4] = jnp.where(first[:n], 0.0, coefs[4])
        coefs[5] = jnp.where(last[:n], 0.0, coefs[5])
        for k in range(6):
            WT[k, r + 1, a : a + n, :] = coefs[k] * inv
        D[r + 1, a : a + n, :] = diag * 1.25
        INV[r + 1, a : a + n, :] = inv

    def set_rhs(r, a=PAD, n=C):
        inv = INV[r + 1, a : a + n, :]
        at = slice(a - PAD, a - PAD + n)
        t, tn = near(W0, 3, r, a, n)
        tn[4] = jnp.where(first[:n], 0.0, tn[4])
        tn[5] = jnp.where(last[:n], 0.0, tn[5])
        advect = vel_ref[0, r, at] * (tn[3] - tn[2]) + vel_ref[1, r, at] * (tn[1] - tn[0]) + vel_ref[2, r, at] * (tn[5] - tn[4])
        spread_t = tn[0] + tn[1] + tn[2] + tn[3] + tn[4] + tn[5] - 6.0 * t
        t_next = t + 0.125 * advect + 0.1 * spread_t
        tn_ref[r, at] = t_next
        B[0, r + 1, a : a + n, :] = (mis_ref[0, r, at] + t_next) * inv
        B[1, r + 1, a : a + n, :] = mis_ref[1, r, at] * inv
        B[2, r + 1, a : a + n, :] = mis_ref[2, r, at] * inv

    def change(buf, c, r, lo=PAD, width=C):
        x, xn = near(buf, c, r, lo, width)
        t = B[c, r + 1, lo : lo + width, :] - 0.8 * x
        for k in range(6):
            t = t + WT[k, r + 1, lo : lo + width, :] * xn[k]
        return x, t

    def sweep_to(dst, src, c, r, a, n):
        x, t = change(src, c, r, a, n)
        dst[c, q(r), a : a + n, :] = x + t

    outer = [(lo, PAD), (hi - PAD, PAD)]
    outer_own = [(PAD, PAD // 2), (hi - PAD, PAD // 2)]
    calm = range(1, R - 1)
    calmer = range(2, R - 2)
    rest = lambda some, which: [r for r in some if r not in which]
    for r in calm:
        set_weights(r)
        set_rhs(r)
    for r in calm:
        for c in range(3):
            sweep_to(U1, W0, c, r, PAD, C)
    for r in calmer:
        for c in range(3):
            sweep_to(U2, U1, c, r, lo, span)

    for item in round0:
        item.arrive()
    for c in range(4):
        W0[c, inner, PAD - 1, :] = L0[0, c]
        W0[c, inner, PAD + C, :] = L0[1, c]
    for n in range(3):
        W0[4, inner, PAD - 1 - n, :] = L0[0, 4 + n]
        W0[4, inner, PAD + C + n, :] = L0[1, 4 + n]
    for n, (di, dj) in enumerate(corners):
        rr, cc = (R if dj < 0 else -1), PAD + (C if di < 0 else -1)
        def place_corner(n=n, di=di, dj=dj, rr=rr, cc=cc):
            W0[4, q(rr), cc : cc + 1, :] = LC[n, 0:1]
            W0[4, q(rr), cc - di : cc - di + 1, :] = LC[n, 1:2]
            W0[4, q(rr - dj), cc : cc + 1, :] = LC[n, 2:3]
        pl.when(inside(-dj))(place_corner)

    @pl.when(j == 0)
    def _():
        W0[:, q(-1)] = jnp.zeros_like(W0[:, q(-1)])
        W0[4, q(-3) : q(-1)] = jnp.ones_like(W0[4, q(-3) : q(-1)])

    @pl.when(j == nj - 1)
    def _():
        W0[:, q(R)] = jnp.zeros_like(W0[:, q(R)])
        W0[4, q(R + 1) : q(R + 3)] = jnp.ones_like(W0[4, q(R + 1) : q(R + 3)])

    for r in rest(range(-1, R + 1), calm):
        set_weights(r)
    for r in calm:
        for a, n in outer:
            set_weights(r, a, n)
    for n, (r, k) in enumerate(((-2, 3), (R + 1, 2))):
        coefs, diag, inv = faces(r)
        WF[0, n, lo:hi, :] = coefs[k] * inv
        WF[1, n, lo:hi, :] = coefs[k]
    for r in rest(range(R), calm):
        set_rhs(r)
    for r in calm:
        for a, n in outer_own:
            set_rhs(r, a, n)

    @pl.when(j == 0)
    def _():
        WT[2, 1] = jnp.zeros_like(WT[2, 1])
        WT[:, 0] = jnp.zeros_like(WT[:, 0])

    @pl.when(j == nj - 1)
    def _():
        WT[3, R] = jnp.zeros_like(WT[3, R])
        WT[:, R + 1] = jnp.zeros_like(WT[:, R + 1])

    for c in range(3):
        for r in rest(range(R), calm):
            sweep_to(U1, W0, c, r, PAD, C)
        for r in calm:
            for a, n in outer_own:
                sweep_to(U1, W0, c, r, a, n)

    def residual(c, r):
        x, t = change(U2, c, r, lo, span)
        U3[c, q(r), lo:hi, :] = x + t
        return D[r + 1, lo:hi, :] * t

    def part(c, slot):
        width = NC + 1
        place = lambda buf, start, size: lambda rad: buf.at[rad + 1, c, :, pl.ds(start, size)]
        return relay(slot, {
            -1: CP.at[c, :, pl.ds(strip - 1, width)],
            0: CP.at[c, :, pl.ds(strip - 1, cols + 2)],
            1: CP.at[c, :, pl.ds(strip + cols - NC, width)],
        }, {
            -1: place(GE, strip - 1 + cols, width),
            0: place(GO, strip - 1, cols + 2),
            1: place(GW, strip - NC, width),
        })

    wide_c = span // 2
    slot = 10 + legs
    coarse_res = []
    for c in range(3):
        U2[c, q(-1), mid, :] = WT[3, 0, mid, :] * U1[c, q(0), mid, :]
        U2[c, q(R), mid, :] = WT[2, R + 1, mid, :] * U1[c, q(R - 1), mid, :]
        for r in rest(range(R), calmer):
            sweep_to(U2, U1, c, r, lo, span)
        for r in calmer:
            for a, n in outer:
                sweep_to(U2, U1, c, r, a, n)
        for r, k, p in ((-2, 3, 0), (R + 1, 2, rows + 1)):
            other = -1 if r < 0 else R
            x = U2[c, q(other), lo:hi, :]
            U3[c, q(r), lo:hi, :] = WF[0, int(p > 0), lo:hi, :] * x
            RS[c, p] = WF[1, int(p > 0), lo:hi, :] * x + residual(c, other)
        for p in range(rows):
            RS[c, p + 1] = residual(c, 2 * p) + residual(c, 2 * p + 1)
        pair = lambda p: RS[c, p + 1, pl.ds(0, wide_c, 2), :] + RS[c, p + 1, pl.ds(1, wide_c, 2), :]
        for r, a, b in [(r, r, r + half) for r in range(half)] + [(half, rows, -1)]:
            CP[c, r, strip - 2 : strip - 2 + wide_c, :] = halves(pair(a), pair(b))
        coarse_res.append(part(c, slot))
        slot = slot + legs
        if c == 0:
            visc_direct.arrive()
            visc_onward.start()

    near_cells = [(0, 1), (0, 2), (1, 1), (1, 0), (2, 0)]
    band = pl.ds(PAD - 1, C + 2)
    for n, (di, dj) in enumerate(corners):
        r0, c0 = (0 if dj < 0 else R - 1), PAD + (0 if di < 0 else C - 1)
        for m, (a, b) in enumerate(near_cells):
            for c in range(3):
                at = c0 + di * b
                SD[n, 3 * m + c : 3 * m + c + 1] = U3[c, q(r0 + dj * a), at : at + 1, :]
    fine = []
    for c in range(3):
        for n in range(3):
            SX[0, c, n] = U3[c, q(-1) : q(R + 1), PAD - n, :]
            SX[1, c, n] = U3[c, q(-1) : q(R + 1), PAD + C - 1 + n, :]
        group = [
            Bundle(None, None, [copy(slot, SX.at[0, c], LX.at[1, c], west, j), copy(slot + 1, SX.at[1, c], LX.at[0, c], east, j)]),
            Bundle(inside(-1), inside(1), [
                copy(slot + 2, U3.at[c, pl.ds(q(-2), 3), band], LR.at[1, c, :, band], i, j - 1),
            ] + (diagonal(slot + 4, SD, LD, 15, -1) if c == 0 else [])),
            Bundle(inside(1), inside(-1), [
                copy(slot + 3, U3.at[c, pl.ds(q(R - 1), 3), band], LR.at[0, c, :, band], i, j + 1),
            ] + (diagonal(slot + 4, SD, LD, 15, 1) if c == 0 else [])),
        ]
        slot = slot + (8 if c == 0 else 4)
        fine.append(group)

    visc_onward.arrive()

    lane_c = lane[:C]

    def repack(get, p):
        s, r = p // rows, p % rows
        a, b = get(s, r % half), get(s + nj // 2, r % half)
        if r >= half:
            a = pltpu.roll(a, LAT - 1, 1)
        else:
            b = pltpu.roll(b, 1, 1)
        return jnp.where(even[: a.shape[0]], a, b)

    def coarse_near(buf, c, p, lo=PAD, width=C):
        part = even[:width]
        block = lambda place, off=0: buf[c, place, lo + off : lo + off + width, :]
        x = block(p)
        below = block(p - 1) if p > 0 else jnp.where(part, 0.0, pltpu.roll(block(packed - 1), 1, 1))
        above = block(p + 1) if p < packed - 1 else jnp.where(part, pltpu.roll(block(0), LAT - 1, 1), 0.0)
        return x, [block(p, -1), block(p, 1), below, above, pltpu.roll(x, 2, 1), pltpu.roll(x, LAT - 2, 1)]

    for p in range(packed):
        CG[0, p] = repack(lambda s, r: LV[s, r], p)
    for p in range(packed):
        v, vn = coarse_near(CG, 0, p)
        vn[4] = jnp.where(lane_c < 2, 0.0, vn[4])
        vn[5] = jnp.where(lane_c >= LAT - 2, 0.0, vn[5])
        coefs = [(v + item) * 0.5 for item in vn]
        diag = coefs[0] + coefs[1] + coefs[2] + coefs[3] + coefs[4] + coefs[5]
        inv = 0.8 / diag
        coefs[4] = jnp.where(lane_c < 2, 0.0, coefs[4])
        coefs[5] = jnp.where(lane_c >= LAT - 2, 0.0, coefs[5])
        for k in range(6):
            CW[k, p] = coefs[k] * inv
        CW[6, p] = 4.0 * inv

    for r in range(half + 1):
        for c in range(3):
            GO[j + 1, c, r] = CP[c, r]

    col = lax.broadcasted_iota(jnp.int32, (C, LAT), 0)
    own = (col >= strip - 1) & (col <= strip + cols)
    before, after = col <= strip, col >= strip + cols - 1

    def total(s, c, p):
        x = jnp.where(own, GO[s + 1, c, p], 0.0)
        return x + jnp.where(before, GW[s + 1, c, p], 0.0) + jnp.where(after, GE[s + 1, c, p], 0.0)

    even_c = even[:C]

    def coarse_part(s, c, r):
        b = total(s, c, r)
        if r == 0 and s > 0:
            b = b + jnp.where(even_c, total(s - 1, c, half), 0.0)
        if r == half - 1 and s < nj - 1:
            b = b + jnp.where(even_c, 0.0, total(s + 1, c, half))
        return b

    def coarse_sweep(src, dst, rim):
        near_rim = 2 * rim <= PAD and cols % 8 == 0
        lo = 2 * strip - PAD // 2 if near_rim else PAD
        width = cols + PAD if near_rim else C
        for p in range(packed):
            for c in range(3):
                x, xn = coarse_near(src, c, p, lo, width)
                t = CB[c, p, lo - PAD : lo - PAD + width, :] + 0.2 * x
                for k in range(6):
                    t = t + CW[k, p, lo - PAD : lo - PAD + width, :] * xn[k]
                dst[c, p, lo : lo + width, :] = t

    def hand_on(c):
        coarse_res[c][0].arrive()
        coarse_res[c][1].start()

    hand_on(0)
    for c in range(3):
        for item in fine[c]:
            item.start()
    hand_on(1)
    hand_on(2)
    for c in range(3):
        coarse_res[c][1].arrive()
    for p in range(packed):
        for c in range(3):
            b = repack(lambda s, r: coarse_part(s, c, r), p) * CW[6, p]
            CB[c, p] = b
            EA[c, p, PAD : PAD + C, :] = b
    src, dst = EA, EB
    for number in range(NC - 1):
        coarse_sweep(src, dst, NC - 1 - number)
        src, dst = dst, src
    wide = EX.shape[2] // 2
    start = 2 * strip - PAD // 2
    for m in range(-1, rows + 1):
        at = rows * j + m
        upper = (at >= packed).astype(jnp.int32)
        valid = parity[:wide] == upper
        for c in range(3):
            x = src[c, lax.rem(at + packed, packed), start : start + wide, :]
            other = jnp.where(upper == 1, pltpu.roll(x, LAT - 1, 1), pltpu.roll(x, 1, 1))
            x = jnp.where(valid, x, other)
            EX[c, m + 1, pl.ds(0, wide, 2), :] = x
            EX[c, m + 1, pl.ds(1, wide, 2), :] = x

    def from_above(c):
        for n in range(3):
            U3[c, q(R - 2 + n), band, :] += LR[1, c, n, band, :]

    def from_below(c):
        for n in range(3):
            U3[c, q(-1 + n), band, :] += LR[0, c, n, band, :]

    def add_corner(c, n, di, dj):
        r0, c0 = (R if dj < 0 else -1), PAD + (C if di < 0 else -1)
        for m, (a, b) in enumerate(near_cells):
            at = c0 + di * b
            U3[c, q(r0 + dj * a), at : at + 1, :] += LD[n, 3 * m + c : 3 * m + c + 1]

    for c in range(3):
        for item in fine[c]:
            item.arrive()
            item.leave()
        for n in range(3):
            U3[c, q(-1) : q(R + 1), PAD + C - n, :] += LX[1, c, n]
            U3[c, q(-1) : q(R + 1), PAD - 1 + n, :] += LX[0, c, n]

        @pl.when(j < nj - 1)
        def _():
            from_above(c)
            for n, (di, dj) in enumerate(corners):
                if dj < 0:
                    add_corner(c, n, di, dj)

        @pl.when(j > 0)
        def _():
            from_below(c)
            for n, (di, dj) in enumerate(corners):
                if dj > 0:
                    add_corner(c, n, di, dj)

    for r in range(-1, R + 1):
        for c in range(3):
            x = EX[c, r // 2 + 1, lo:hi, :]
            xn = [
                EX[c, r // 2 + 1, lo - 1 : hi - 1, :],
                EX[c, r // 2 + 1, lo + 1 : hi + 1, :],
                EX[c, (r - 1) // 2 + 1, lo:hi, :],
                EX[c, (r + 1) // 2 + 1, lo:hi, :],
                pltpu.roll(x, 1, 1),
                pltpu.roll(x, LAT - 1, 1),
            ]
            t = U3[c, q(r), lo:hi, :] + 0.2 * x
            for k in range(6):
                t = t + WT[k, r + 1, lo:hi, :] * xn[k]
            U4[c, q(r), lo:hi, :] = t
    for r in range(R):
        for c in range(3):
            x, t = change(U4, c, r)
            out_ref[c, r] = x + t
    for item in round0:
        item.leave()
    for pair in [(visc_direct, visc_onward)] + coarse_res:
        for item in pair:
            item.leave()


def deliver(tn_ref, out_ref, tn_hbm, out_hbm, sems):
    copies = [pltpu.make_async_copy(tn_ref, tn_hbm, sems.at[0]), pltpu.make_async_copy(out_ref, out_hbm, sems.at[1])]
    for item in copies:
        item.start()
    for item in copies:
        item.wait()


def solution(mesh):
    ni, nj = mesh.shape["lon"], mesh.shape["rad"]

    def local(adjoint_temp, viscosity, velocity, misfit_force, adjoint_guess):
        R, C, LAT = adjoint_temp.shape
        half, cols, wide = R // 4, C // 2, C + 2 * PAD
        f32 = jnp.float32
        frame = lambda n, rows: pltpu.VMEM((n, rows, wide, LAT), f32)
        block = lambda *dims: pltpu.VMEM(dims + (C, LAT), f32)
        copies = 26 + 4 * (3 * nj - 1)
        deep = R + 2 * DEEP
        vmem, place = pl.BlockSpec(memory_space=pltpu.VMEM), pl.BlockSpec(memory_space=pl.ANY)
        P8 = half * nj
        results = pl.pallas_call(
            functools.partial(kernel, ni, nj),
            out_shape=(
                pltpu.VMEM(adjoint_temp.shape, f32),
                pltpu.VMEM(adjoint_guess.shape, f32),
            ),
            in_specs=[place] * 5,
            out_specs=(vmem, vmem),
            scratch_shapes=[
                block(3, R), block(3, R), pltpu.SemaphoreType.DMA((5,)),
                frame(5, deep), frame(3, deep), frame(3, deep), frame(4, deep), frame(3, deep),
                frame(6, R + 2), frame(3, R + 2), pltpu.VMEM((R + 2, wide, LAT), f32), pltpu.VMEM((R + 2, wide, LAT), f32), frame(2, 2),
                pltpu.VMEM((3, 2 * half + 2, C + PAD, LAT), f32), block(2 * half),
                block(3, half + 1), pltpu.VMEM((1, half, cols, LAT), f32),
                block(nj + 2, 3, half + 1), block(nj + 2, 3, half + 1), block(nj + 2, 3, half + 1),
                pltpu.VMEM((nj, half, wide, LAT), f32), frame(1, P8), block(7, P8), block(3, P8),
                frame(3, P8), frame(3, P8), frame(3, 2 * half + 2),
                pltpu.VMEM((2, 7, R, LAT), f32), pltpu.VMEM((2, 7, R, LAT), f32),
                pltpu.VMEM((5, 8, LAT), f32), pltpu.VMEM((5, 8, LAT), f32),
                pltpu.VMEM((2, 3, 3, R + 2, LAT), f32), pltpu.VMEM((2, 3, 3, R + 2, LAT), f32),
                pltpu.VMEM((2, 3, 3, wide, LAT), f32),
                pltpu.VMEM((5, 16, LAT), f32), pltpu.VMEM((5, 16, LAT), f32),
                pltpu.SemaphoreType.DMA((copies,)), pltpu.SemaphoreType.DMA((copies,)),
            ],
            compiler_params=pltpu.CompilerParams(collective_id=0, has_side_effects=True),
        )(adjoint_temp, viscosity, velocity, misfit_force, adjoint_guess)
        return pl.pallas_call(
            deliver,
            out_shape=(jax.ShapeDtypeStruct(adjoint_temp.shape, f32), jax.ShapeDtypeStruct(adjoint_guess.shape, f32)),
            in_specs=[vmem] * 2,
            out_specs=(place, place),
            scratch_shapes=[pltpu.SemaphoreType.DMA((2,))],
        )(*[pltpu.with_memory_space_constraint(item, pltpu.VMEM) for item in results])

    flat = P("rad", "lon", None)
    full = P(None, "rad", "lon", None)
    return jax.shard_map(local, mesh=mesh, in_specs=(flat, flat, full, full, full), out_specs=(flat, full), check_vma=False)
```
